32 devices in a mesh: groups: 2 (over y), rows: 4 (over z), cols: 4 (over x, core).
Axes of the slice: x: 2, y: 2, z: 4, core: 2. Of those that a mesh axis runs over, the one named last changes fastest.
Arguments:
- pixels: bfloat16 [128, 64, 128], P(('groups', 'rows'), 'cols'), parts along dimension 0, may hold values from -6 to 6
- cotangent: bfloat16 [128, 64, 128], P(('groups', 'rows'), 'cols'), parts along dimension 0, may hold values from -6 to 6
- w_in: bfloat16 [128, 512], replicated, may hold values from -0.5 to 0.5
- w_out: bfloat16 [256, 128], replicated, may hold values from -0.375 to 0.375
- decay_rates: float32 [4, 256], replicated, may hold values from 0.0015625 to 0.03, as said below
- step_sizes: float32 [4, 128, 64], P(None, ('groups', 'rows'), 'cols'), parts along dimension 1, may hold values from 0.25 to 128, as said below
Outputs:
- grad_pixels: bfloat16 [128, 64, 128], P(('groups', 'rows'), 'cols'), parts along dimension 0
- grad_in: float32 [256, 512], P(('groups', 'rows'), 'cols'), parts along dimension 0
- grad_out: float32 [512, 128], P(('groups', 'rows'), 'cols'), parts along dimension 0
The draws below stay inside these ranges and needn't reach their ends.
There are 2 independent parts, one for each index of `groups`. The reference program is written for one: setup_inputs(seed, part) draws one part's arguments, and reference() takes and returns one part's arrays. A program takes and returns all parts, laid end to end along the dimension named above; an argument that names none is the same for every part. Nothing has to cross between parts.
Inputs may be any that keep to these rules, and one draw needn't show every extreme that they name: `decay_rates`: positive decay rates. `step_sizes`: positive step sizes.
All inputs are finite; a program needn't handle non-finite values.
Results may differ from the reference program's by a relative error of at most 0.005.
Values sent between devices are 32-bit elements; how exact they have to be, the bound alone decides.
No kernel may reach another device: no remote copies, remote signals or barrier semaphores. Data moves between devices by JAX's collectives and lax.ppermute only.
A program may use at most 64 MiB of HBM per device.

```python
import math
import jax
import jax.numpy as jnp
from jax import lax

C = 128
E = 256
PR = 16
PC = 16
IMAGE_VERTICAL = 64
IMAGE_WIDTH_SPAN = 64


def draw_decay_rates(key, part):
    window_span = max(IMAGE_VERTICAL, IMAGE_WIDTH_SPAN)
    lowest = 0.1 / window_span
    return jnp.exp(jax.random.uniform(key, (4, E), jnp.float32, math.log(lowest), math.log(0.03))).astype(jnp.float32)


def draw_step_sizes(key, part):
    window_span = max(IMAGE_VERTICAL, IMAGE_WIDTH_SPAN)
    patch_seed, smooth_seed, spike_seed, vertical_seed = jax.random.split(key, 4)
    tiles = jnp.exp(jax.random.uniform(patch_seed, (4, IMAGE_VERTICAL // PR, IMAGE_WIDTH_SPAN // PC), jnp.float32, math.log(0.5), math.log(2.0)))
    patch_arrangement = jnp.repeat(jnp.repeat(tiles, PR, axis=1), PC, axis=2)
    smooth_perturbation = jax.random.uniform(smooth_seed, (4, IMAGE_VERTICAL, IMAGE_WIDTH_SPAN), jnp.float32, 0.5, 1.5)
    nearby_spike = jax.random.uniform(spike_seed, (4, IMAGE_VERTICAL, IMAGE_WIDTH_SPAN), jnp.float32) < 4.0 / window_span
    spike_span = window_span * jax.random.uniform(vertical_seed, (4, IMAGE_VERTICAL, IMAGE_WIDTH_SPAN), jnp.float32, 0.5, 2.0)
    return jnp.where(nearby_spike, spike_span, patch_arrangement * smooth_perturbation).astype(jnp.float32)


def spiked(entries, rng, source, target, shards_of, factor):
    owner, partner = [(jnp.arange(entries.shape[axis_at]) // (entries.shape[axis_at] // shards_of)).reshape([-1 if axis == axis_at else 1 for axis in range(entries.ndim)]) for axis_at in (source, target)]
    chosen = jax.random.permutation(rng, shards_of)[partner]
    strong = (owner == chosen) | (owner == (partner + shards_of // 2) % shards_of)
    return jnp.where(strong, factor * entries, entries)


def shard_levels(key, shape, cuts, smallest, top_value):
    gain = 1.0
    for axis_at, shards_of in cuts:
        draws = jax.random.uniform(jax.random.fold_in(jax.random.fold_in(key, 6), axis_at), (shards_of,), jnp.float32, smallest / len(cuts), top_value / len(cuts))
        gain = gain * jnp.repeat(jnp.exp(draws), shape[axis_at] // shards_of).reshape((-1,) + (1,) * (len(shape) - 1 - axis_at))
    return gain


def noise(stream_key, dims, spread, reach, cuts=(), kind=jnp.bfloat16):
    loudness = shard_levels(stream_key, dims, cuts, -0.22, 0.18) if cuts else 1.0
    entries = jax.random.normal(stream_key, dims, jnp.float32) * spread * loudness
    return jnp.minimum(jnp.maximum(entries, -reach), reach).astype(kind)


def heavy_noise(key, extent, scale, limit, cuts, heavy, kind=jnp.bfloat16):
    entries = scale * jax.random.normal(key, extent, jnp.float32)
    if cuts:
        entries = entries * shard_levels(key, extent, cuts, -0.22, 0.18)
    return jnp.clip(spiked(entries, jax.random.fold_in(key, 3), *heavy), -limit, limit).astype(kind)


def setup_inputs(seed: int = 0, part: int = 0) -> dict:
    key_list = jax.random.split(jax.random.key(seed), 7)
    own_keys = jax.random.split(jax.random.fold_in(key_list[6], part), 7)
    pixels = heavy_noise(own_keys[0], (IMAGE_VERTICAL, IMAGE_WIDTH_SPAN, C), 1.0, 6.0, ((0, 4), (1, 4)), (0, 2, 4, 2.0))
    cotangent = heavy_noise(own_keys[1], (IMAGE_VERTICAL, IMAGE_WIDTH_SPAN, C), 1.0, 6.0, ((0, 4), (1, 4)), (1, 2, 4, 2.0))
    w_in = noise(key_list[2], (C, 2 * E), C ** -0.5, 0.5)
    w_out = noise(key_list[3], (E, C), E ** -0.5, 0.375)
    decay_rates = draw_decay_rates(jax.random.fold_in(key_list[6], 71), part)
    step_sizes = draw_step_sizes(jax.random.fold_in(jax.random.fold_in(key_list[6], part), 71), part)
    return dict(pixels=pixels, cotangent=cotangent, w_in=w_in, w_out=w_out, decay_rates=decay_rates, step_sizes=step_sizes)


line_order = ((1, False), (1, True), (0, False), (0, True))

def affine(earlier_map, later_map):
    return (earlier_map[0] * later_map[0], later_map[0] * earlier_map[1] + later_map[1])

def shift_in(values, line_axis, backward, filler):
    length = values.shape[line_axis]
    if backward:
        return jnp.concatenate([filler, lax.slice_in_dim(values, 0, length - 1, axis=line_axis)], axis=line_axis)
    return jnp.concatenate([lax.slice_in_dim(values, 1, length, axis=line_axis), filler], axis=line_axis)

def silu_slope(values):
    sigma = jax.nn.sigmoid(values)
    return sigma * (1.0 + values * (1.0 - sigma))

def reference(pixels, cotangent, w_in, w_out, decay_rates, step_sizes):
    height, breadth, channels = pixels.shape
    expand = w_out.shape[0]
    block_size = 32
    pixel_count = height * breadth
    flat_in = pixels.reshape(pixel_count, channels)
    flat_cot = cotangent.reshape(pixel_count, channels)
    contract_rows = (((0,), (0,)), ((), ()))
    contract_cols = (((1,), (1,)), ((), ()))

    def one_block(accum, offset):
        w_inner = lax.dynamic_slice_in_dim(w_in, offset, block_size, 1)
        w_gate = lax.dynamic_slice_in_dim(w_in, offset + expand, block_size, 1)
        w_back = lax.dynamic_slice_in_dim(w_out, offset, block_size, 0)
        rate_block = lax.dynamic_slice_in_dim(decay_rates, offset, block_size, 1)
        inner_part = jnp.dot(flat_in, w_inner, preferred_element_type=jnp.float32).reshape(height, breadth, block_size)
        gate_part = jnp.dot(flat_in, w_gate, preferred_element_type=jnp.float32).reshape(height, breadth, block_size)
        back_grad = lax.dot_general(flat_cot, w_back, contract_cols, preferred_element_type=jnp.float32).reshape(height, breadth, block_size)
        source = jax.nn.silu(inner_part)
        gated = jax.nn.silu(gate_part)
        seed_grad = back_grad * gated
        total = jnp.zeros_like(source)
        grad_source = jnp.zeros_like(source)
        for line_no in range(4):
            line_axis, backward = line_order[line_no]
            scaled = rate_block[line_no][None, None, :] * step_sizes[line_no][:, :, None]
            decay_now = jnp.exp(-scaled)
            weight = jnp.sqrt(-jnp.expm1(-2.0 * scaled))
            states = lax.associative_scan(affine, (decay_now, weight * source), reverse=backward, axis=line_axis)[1]
            carried = lax.associative_scan(affine, (decay_now, decay_now * seed_grad), reverse=not backward, axis=line_axis)[1]
            filler = jnp.zeros_like(lax.slice_in_dim(carried, 0, 1, axis=line_axis))
            total = total + states
            grad_source = grad_source + weight * (seed_grad + shift_in(carried, line_axis, backward, filler))
        out_state = (total * gated).astype(jnp.bfloat16).reshape(pixel_count, block_size)
        grad_inner = (grad_source * silu_slope(inner_part)).astype(jnp.bfloat16).reshape(pixel_count, block_size)
        grad_gate = (back_grad * total * silu_slope(gate_part)).astype(jnp.bfloat16).reshape(pixel_count, block_size)
        part_inner = lax.dot_general(flat_in, grad_inner, contract_rows, preferred_element_type=jnp.float32)
        part_gate = lax.dot_general(flat_in, grad_gate, contract_rows, preferred_element_type=jnp.float32)
        part_out = lax.dot_general(out_state, flat_cot, contract_rows, preferred_element_type=jnp.float32)
        accum = accum + lax.dot_general(grad_inner, w_inner, contract_cols, preferred_element_type=jnp.float32)
        accum = accum + lax.dot_general(grad_gate, w_gate, contract_cols, preferred_element_type=jnp.float32)
        return (accum, (part_inner, part_gate, part_out))
    offsets = jnp.arange(expand // block_size, dtype=jnp.int32) * block_size
    start_accum = jnp.zeros((pixel_count, channels), jnp.float32)
    accum, pieces = lax.scan(one_block, start_accum, offsets)
    grad_in = jnp.concatenate([pieces[0].transpose(1, 0, 2).reshape(channels, expand), pieces[1].transpose(1, 0, 2).reshape(channels, expand)], axis=1)
    grad_out = pieces[2].reshape(expand, channels)
    grad_pixels = (flat_cot.astype(jnp.float32) + accum).astype(jnp.bfloat16).reshape(height, breadth, channels)
    return (grad_pixels, grad_in, grad_out)
```

```python
import functools

import jax
import jax.numpy as jnp
from jax import lax
from jax.experimental import pallas as pl
from jax.experimental.pallas import tpu as pltpu
from jax.sharding import PartitionSpec as P

F32 = jnp.float32
BF16 = jnp.bfloat16
contract_rows = (((0,), (0,)), ((), ()))
contract_cols = (((1,), (1,)), ((), ()))
VMEM_LIMIT = 20 * 1024 * 1024
PAD = 128


def vmem_call(body, out_shape, scratch=(), flops=0, moved=0, space=pltpu.VMEM):
    spec = pl.BlockSpec(memory_space=pltpu.VMEM)
    given = pl.BlockSpec(memory_space=space)
    return lambda *operands: pl.pallas_call(
        body,
        out_shape=out_shape,
        in_specs=[given] * len(operands),
        out_specs=jax.tree.map(lambda _: spec, out_shape),
        scratch_shapes=scratch,
        compiler_params=pltpu.CompilerParams(vmem_limit_bytes=VMEM_LIMIT),
        cost_estimate=pl.CostEstimate(flops=flops, bytes_accessed=moved, transcendentals=0),
    )(*operands)


def get(ref, rows):
    return jnp.concatenate([ref[k, rows, :] for k in range(ref.shape[0])], axis=1)


def put(ref, rows, value):
    for k in range(ref.shape[0]):
        ref[k, rows, :] = value[:, 128 * k : 128 * k + 128]


def sigmoid(value):
    return 1.0 / (1.0 + jnp.exp(-value))


def decay_pair(rate, step):
    decay = jnp.exp(-(rate * step))
    rest = 1.0 - decay * decay
    return decay, rest * lax.rsqrt(rest)


def edges_body(px_in, ct_in, wi_in, wo_in, rt_in, ss_in, e_cols, e_rows, px, ct, wi, rt, mixed, back, src, seed, dec, wgt, wo, ss, sems):
    pairs = ((px_in, px), (wi_in, wi), (ct_in, ct), (wo_in, wo), (ss_in, ss), (rt_in, rt))
    copies = [pltpu.make_async_copy(a, b, sems.at[k]) for k, (a, b) in enumerate(pairs)]
    for copy in copies:
        copy.start()
    height, breadth, channels = px.shape
    expand = wo.shape[0]
    count = height * breadth
    copies[0].wait()
    copies[1].wait()
    both = jnp.dot(px[...].reshape(count, channels), wi[...], preferred_element_type=F32)
    mixed[...] = both
    copies[2].wait()
    copies[3].wait()
    cot = ct[...].reshape(count, channels)
    bg = lax.dot_general(cot, wo[...], contract_cols, preferred_element_type=F32)
    back[...] = bg
    inner, gate = both[:, :expand], both[:, expand:]
    put(src, slice(None), inner * sigmoid(inner))
    put(seed, slice(None), bg * (gate * sigmoid(gate)))
    copies[4].wait()
    copies[5].wait()

    for axis, payload in ((0, e_cols), (1, e_rows)):
        one, two = 2 * axis, 2 * axis + 1
        length = breadth if axis == 0 else height
        lines = height if axis == 0 else breadth

        def at(ref, i):
            return get(ref, pl.ds(i, lines, stride=length) if axis == 0 else pl.ds(i * lines, lines))

        steps = [ss[d] if axis == 0 else jnp.transpose(ss[d]) for d in (one, two)]
        rates = [rt[d : d + 1, :] for d in (one, two)]
        fwd = jnp.zeros((lines, expand), F32)
        adj = jnp.zeros((lines, expand), F32)
        for i in range(length):
            rows = slice(i * lines, (i + 1) * lines)
            d1, w1 = decay_pair(rates[0], steps[0][:, i : i + 1])
            d2, w2 = decay_pair(rates[1], steps[1][:, i : i + 1])
            dec[one, rows, :] = d1
            wgt[one, rows, :] = w1
            dec[two, rows, :] = d2
            wgt[two, rows, :] = w2
            fwd = d1 * fwd + w1 * at(src, i)
            adj = d2 * (adj + at(seed, i))
        payload[0, :, 0:expand] = fwd
        payload[0, :, expand : 2 * expand] = adj
        fwd = jnp.zeros((lines, expand), F32)
        adj = jnp.zeros((lines, expand), F32)
        for i in reversed(range(length)):
            rows = slice(i * lines, (i + 1) * lines)
            d1, d2, w2 = dec[one, rows, :], dec[two, rows, :], wgt[two, rows, :]
            fwd = d2 * fwd + w2 * at(src, i)
            adj = d1 * (adj + at(seed, i))
        payload[1, :, 0:expand] = adj
        payload[1, :, expand : 2 * expand] = fwd
        lane = lax.broadcasted_iota(jnp.int32, (lines, PAD), 1)
        sums = [jnp.sum(s, axis=1, keepdims=True) for s in steps]
        for way in (0, 1):
            payload[way, :, 2 * expand :] = jnp.where(lane < PAD // 2, sums[0], sums[1])


def local_body(px, ct, mixed, back, src, seed, dec, wgt, s_loc, g_loc, pre, suf, m_in, m_gate, gated, x_t, c_t):
    height, breadth, channels = px.shape
    expand = src.shape[0] * 128
    count = height * breadth
    inner, gate = mixed[:, :expand], mixed[:, expand:]
    s_in = sigmoid(inner)
    m_in[...] = s_in * (1.0 + inner * (1.0 - s_in))
    s_gate = sigmoid(gate)
    gated[...] = gate * s_gate
    m_gate[...] = back[...] * (s_gate * (1.0 + gate * (1.0 - s_gate)))
    x_t[...] = jnp.transpose(px[...].reshape(count, channels).astype(F32)).astype(BF16)
    c_t[...] = jnp.transpose(ct[...].reshape(count, channels).astype(F32)).astype(BF16)
    for axis in (0, 1):
        one, two = 2 * axis, 2 * axis + 1
        length = breadth if axis == 0 else height
        lines = height if axis == 0 else breadth

        def where(i):
            if axis == 0:
                return pl.ds(i, lines, stride=length)
            return pl.ds(i * lines, lines)

        def go(order, a, b, first):
            state = jnp.zeros((lines, expand), F32)
            carried = jnp.zeros((lines, expand), F32)
            upto = jnp.ones((lines, expand), F32)
            after = jnp.ones((lines, expand), F32)
            for i in order:
                rows = slice(i * lines, (i + 1) * lines)
                da, wa, db, wb = dec[a, rows, :], wgt[a, rows, :], dec[b, rows, :], wgt[b, rows, :]
                state = da * state + wa * get(src, where(i))
                upto = upto * da
                adjoint = get(seed, where(i)) + carried
                carried = db * adjoint
                put(pre.at[a], where(i), upto)
                put(suf.at[b], where(i), wb * after)
                after = after * db
                grad = wb * adjoint
                if not first:
                    state_sum, grad = get(s_loc, where(i)) + state, get(g_loc, where(i)) + grad
                else:
                    state_sum = state
                put(s_loc, where(i), state_sum)
                put(g_loc, where(i), grad)

        go(range(length), one, two, axis == 0)
        go(reversed(range(length)), two, one, False)


def entering(axis, rates, parts):
    count, mine = len(parts) + 1, lax.axis_index(axis)
    expand = rates[0].shape[1]
    lines = parts[0].shape[0]
    sums = [
        jnp.concatenate([jnp.broadcast_to(part[:, c : c + 1], (lines, expand)) for c in (2 * expand, 2 * expand + PAD // 2)], axis=1)
        for part in parts
    ]
    both = jnp.concatenate(rates, axis=1)
    below = jnp.zeros((lines, 2 * expand), F32)
    above = jnp.zeros((lines, 2 * expand), F32)
    for k in range(1, count):
        place = mine ^ k
        between = jnp.zeros((lines, 2 * expand), F32)
        for m in range(1, count):
            if m == k:
                continue
            middle = mine ^ m
            inside = ((middle - mine) * (middle - place) < 0).astype(F32)
            between = between + inside * sums[m - 1]
        value = jnp.exp(-both * between) * parts[k - 1][:, : 2 * expand]
        lower = (place < mine).astype(F32)
        below = below + lower * value
        above = above + (1.0 - lower) * value
    return below, above


def join_body(shape, split, counts, rt, *refs):
    height, breadth = shape
    n_cols, n_rows = counts[0] - 1, counts[1] - 1
    from_cols, from_rows = refs[:n_cols], refs[n_cols : n_cols + n_rows]
    s_loc, g_loc, pre, suf, m_in, m_gate, gated, x_t, c_t, mix = refs[n_cols + n_rows : n_cols + n_rows + 10]
    outs = refs[n_cols + n_rows + 10 :]
    expand = s_loc.shape[0] * 128
    out_state = outs[-1]
    grads = outs[:-1]
    rates = [rt[d : d + 1, :] for d in range(4)]
    below, above = entering("rows", rates[2:], [r[...] for r in from_rows])
    f2, a3, a2, f3 = below[:, :expand], below[:, expand:], above[:, :expand], above[:, expand:]
    below, above = entering("cols", rates[:2], [r[...] for r in from_cols])
    for h in range(height):
        rows = slice(h * breadth, (h + 1) * breadth)
        f0, a1 = below[h : h + 1, :expand], below[h : h + 1, expand:]
        a0, f1 = above[h : h + 1, :expand], above[h : h + 1, expand:]
        total, grad = get(s_loc, rows), get(g_loc, rows)
        for d, (state_in, adjoint_in) in enumerate(((f0, a0), (f1, a1), (f2, a2), (f3, a3))):
            total = total + get(pre.at[d], rows) * state_in
            grad = grad + get(suf.at[d], rows) * adjoint_in
        out_state[rows, :] = (total * gated[rows, :]).astype(BF16)
        mix[rows, :expand] = (grad * m_in[rows, :]).astype(BF16)
        mix[rows, expand:] = (total * m_gate[rows, :]).astype(BF16)
    grad_in = jnp.dot(x_t[...], mix[...], preferred_element_type=F32)
    grad_out = jnp.dot(c_t[...], out_state[...], preferred_element_type=F32)
    if not split:
        grads[0][...] = grad_in
        grads[1][...] = grad_out
        return
    packed = grads[0]
    lane = lax.broadcasted_iota(jnp.int32, (16, 128), 1)
    for c in range(4):
        for t in range(2):
            top = grad_out[32 * c : 32 * c + 16, 128 * t : 128 * t + 128]
            bottom = grad_out[32 * c + 16 : 32 * c + 32, 128 * t : 128 * t + 128]
            low = jnp.where(lane < 64, top, pltpu.roll(bottom, 64, 1))
            high = jnp.where(lane < 64, pltpu.roll(top, 64, 1), bottom)
            for k, piece in ((0, low), (1, high)):
                r = 2 * t + k
                packed[c & 1, c >> 1, k, t, 0:32, :] = grad_in[32 * r : 32 * r + 32, 128 * c : 128 * c + 128]
                packed[c & 1, c >> 1, k, t, 32:48, :] = piece


def pixels_body(ct, mix, wi, out):
    height, breadth, channels = ct.shape
    grad = lax.dot_general(mix[...], wi[...], contract_cols, preferred_element_type=F32)
    cot = ct[...].reshape(height * breadth, channels).astype(F32)
    out[...] = (cot + grad).astype(BF16).reshape(height, breadth, channels)


def final_body(mine, other, g_in, g_out):
    total = mine[...] + other[...]
    g_in[...] = total[0:32, :]
    g_out[0:16, :] = total[32:48, 0:64]
    g_out[16:32, :] = total[32:48, 64:128]


def partner(value, axis, bit):
    return lax.ppermute(value, axis, [(i, i ^ bit) for i in range(lax.axis_size(axis))])


def exchange(payload, axis):
    mine = lax.axis_index(axis)
    received = []
    for k in range(1, lax.axis_size(axis)):
        way = ((mine ^ k) < mine).astype(jnp.int32)
        received.append(partner(lax.dynamic_index_in_dim(payload, way, 0, keepdims=False), axis, k))
    return received


def halve(value, axis, bit):
    mine = (lax.axis_index(axis) & bit) // bit
    pick = lambda i: lax.dynamic_index_in_dim(value, i, 0, keepdims=False)
    return pick(mine), partner(pick(1 - mine), axis, bit)


def per_device(pixels, cotangent, w_in, w_out, decay_rates, step_sizes):
    height, breadth, channels = pixels.shape
    expand = w_out.shape[0]
    count = height * breadth
    rows, cols = lax.axis_size("rows"), lax.axis_size("cols")
    full = jax.ShapeDtypeStruct((count, expand), F32)
    tall = jax.ShapeDtypeStruct((expand // 128, count, 128), F32)
    four_tall = jax.ShapeDtypeStruct((4, expand // 128, count, 128), F32)
    four = jax.ShapeDtypeStruct((4, count, expand), F32)
    wide = jax.ShapeDtypeStruct((count, 2 * expand), F32)
    like = lambda a: jax.ShapeDtypeStruct(a.shape, a.dtype)
    e_cols, e_rows, px, ct, wi, rt, mixed, back, src, seed, dec, wgt = vmem_call(
        edges_body,
        (
            jax.ShapeDtypeStruct((2, height, 2 * expand + PAD), F32),
            jax.ShapeDtypeStruct((2, breadth, 2 * expand + PAD), F32),
            like(pixels), like(cotangent), like(w_in), like(decay_rates),
            wide, full, tall, tall, four, four,
        ),
        scratch=[pltpu.VMEM(w_out.shape, BF16), pltpu.VMEM(step_sizes.shape, F32), pltpu.SemaphoreType.DMA((6,))],
        space=pl.ANY,
    )(pixels, cotangent, w_in, w_out, decay_rates, step_sizes)
    turned = jax.ShapeDtypeStruct((channels, count), BF16)
    s_loc, g_loc, pre, suf, m_in, m_gate, gated, x_t, c_t = vmem_call(
        local_body, (tall, tall, four_tall, four_tall, full, full, full, turned, turned)
    )(px, ct, mixed, back, src, seed, dec, wgt)
    from_rows = exchange(e_rows, "rows")
    from_cols = exchange(e_cols, "cols")
    split = rows == 4 and cols == 4 and channels == 128 and expand == 256
    if split:
        grads = (jax.ShapeDtypeStruct((2, 2, 2, 2, 48, 128), F32),)
    else:
        grads = (
            jax.ShapeDtypeStruct((channels, 2 * expand), F32),
            jax.ShapeDtypeStruct((channels, expand), F32),
        )
    outs = vmem_call(
        functools.partial(join_body, (height, breadth), split, (cols, rows)),
        (jax.ShapeDtypeStruct((count, 2 * expand), BF16), *grads, jax.ShapeDtypeStruct((count, expand), BF16)),
    )(rt, *from_cols, *from_rows, s_loc, g_loc, pre, suf, m_in, m_gate, gated, x_t, c_t)
    mix, grads = outs[0], outs[1:-1]
    grad_pixels = vmem_call(pixels_body, jax.ShapeDtypeStruct(pixels.shape, BF16))(ct, mix, wi)
    if split:
        value = grads[0]
        for axis, bit in (("cols", 1), ("cols", 2), ("rows", 1)):
            kept, got = halve(value, axis, bit)
            value = kept + got
        kept, got = halve(value, "rows", 2)
        grad_in, grad_out = vmem_call(
            final_body, (jax.ShapeDtypeStruct((32, 128), F32), jax.ShapeDtypeStruct((32, 64), F32))
        )(kept, got)
        return grad_pixels, grad_in, jnp.transpose(grad_out)
    full_in, full_out = grads[0], jnp.transpose(grads[1])
    full_in = lax.psum_scatter(full_in, "cols", scatter_dimension=1, tiled=True)
    full_out = lax.psum_scatter(full_out, "cols", scatter_dimension=1, tiled=True)
    return (
        grad_pixels,
        lax.psum_scatter(full_in, "rows", scatter_dimension=0, tiled=True),
        lax.psum_scatter(full_out, "rows", scatter_dimension=0, tiled=True),
    )


def solution(mesh):
    return jax.shard_map(
        per_device,
        mesh=mesh,
        in_specs=(
            P(("groups", "rows"), "cols", None),
            P(("groups", "rows"), "cols", None),
            P(),
            P(),
            P(),
            P(None, ("groups", "rows"), "cols"),
        ),
        out_specs=(
            P(("groups", "rows"), "cols", None),
            P(("groups", "rows"), "cols"),
            P(("groups", "rows"), "cols"),
        ),
        check_vma=False,
    )
```

```python
import functools

import jax
import jax.numpy as jnp
from jax import lax
from jax.experimental import pallas as pl
from jax.experimental.pallas import tpu as pltpu
from jax.sharding import PartitionSpec as P

F32 = jnp.float32
BF16 = jnp.bfloat16
contract_rows = (((0,), (0,)), ((), ()))
contract_cols = (((1,), (1,)), ((), ()))
VMEM_LIMIT = 6 * 1024 * 1024
PAD = 128


def vmem_call(body, out_shape, scratch=(), given=pltpu.VMEM, kept=True):
    spec = pl.BlockSpec(memory_space=pltpu.VMEM)
    if kept:
        out_shape = jax.tree.map(lambda s: pltpu.VMEM(s.shape, s.dtype), out_shape)

    def call(*operands):
        operands = [pltpu.with_memory_space_constraint(a, given) for a in operands]
        return pl.pallas_call(
            body,
            out_shape=out_shape,
            in_specs=[pl.BlockSpec(memory_space=given)] * len(operands),
            out_specs=jax.tree.map(lambda _: spec, out_shape),
            scratch_shapes=scratch,
            compiler_params=pltpu.CompilerParams(vmem_limit_bytes=VMEM_LIMIT),
            cost_estimate=pl.CostEstimate(flops=0, bytes_accessed=0, transcendentals=0),
        )(*operands)

    return call


def get(ref, rows):
    return jnp.concatenate([ref[k, rows, :] for k in range(ref.shape[0])], axis=1)


def put(ref, rows, value):
    for k in range(ref.shape[0]):
        ref[k, rows, :] = value[:, 128 * k : 128 * k + 128]


def sigmoid(value):
    return 1.0 / (1.0 + jnp.exp(-value))


def decay_pair(rate, step):
    decay = jnp.exp(-(rate * step))
    rest = 1.0 - decay * decay
    return decay, rest * lax.rsqrt(rest)


def edges_body(counts, px_in, ct_in, wi_in, wo_in, rt_in, ss_in, *refs):
    n_cols, n_rows = counts[0] - 1, counts[1] - 1
    sent = (refs[:n_cols], refs[n_cols : n_cols + n_rows])
    px, ct, wi, rt, ss, mixed, back, src, seed, dec, wgt, wo, ways, sems = refs[n_cols + n_rows :]
    pairs = ((px_in, px), (wi_in, wi), (ct_in, ct), (wo_in, wo), (ss_in, ss), (rt_in, rt))
    copies = [pltpu.make_async_copy(a, b, sems.at[k]) for k, (a, b) in enumerate(pairs)]
    for copy in copies:
        copy.start()
    height, breadth, channels = px.shape
    expand = wo.shape[0]
    count = height * breadth
    copies[0].wait()
    copies[1].wait()
    both = jnp.dot(px[...].reshape(count, channels), wi[...], preferred_element_type=F32)
    mixed[...] = both
    copies[2].wait()
    copies[3].wait()
    cot = ct[...].reshape(count, channels)
    bg = lax.dot_general(cot, wo[...], contract_cols, preferred_element_type=F32)
    back[...] = bg
    inner, gate = both[:, :expand], both[:, expand:]
    put(src, slice(None), inner * sigmoid(inner))
    put(seed, slice(None), bg * (gate * sigmoid(gate)))
    copies[4].wait()
    copies[5].wait()

    for axis, name in ((0, "cols"), (1, "rows")):
        payload = ways.at[axis]
        one, two = 2 * axis, 2 * axis + 1
        length = breadth if axis == 0 else height
        lines = height if axis == 0 else breadth

        def at(ref, i):
            return get(ref, pl.ds(i, lines, stride=length) if axis == 0 else pl.ds(i * lines, lines))

        steps = [ss[d] if axis == 0 else jnp.transpose(ss[d]) for d in (one, two)]
        rates = [rt[d : d + 1, :] for d in (one, two)]
        fwd = jnp.zeros((lines, expand), F32)
        adj = jnp.zeros((lines, expand), F32)
        for i in range(length):
            rows = slice(i * lines, (i + 1) * lines)
            d1, w1 = decay_pair(rates[0], steps[0][:, i : i + 1])
            d2, w2 = decay_pair(rates[1], steps[1][:, i : i + 1])
            dec[one, rows, :] = d1
            wgt[one, rows, :] = w1
            dec[two, rows, :] = d2
            wgt[two, rows, :] = w2
            fwd = d1 * fwd + w1 * at(src, i)
            adj = d2 * (adj + at(seed, i))
        payload[0, :, 0:expand] = fwd
        payload[0, :, expand : 2 * expand] = adj
        fwd = jnp.zeros((lines, expand), F32)
        adj = jnp.zeros((lines, expand), F32)
        for i in reversed(range(length)):
            rows = slice(i * lines, (i + 1) * lines)
            d1, d2, w2 = dec[one, rows, :], dec[two, rows, :], wgt[two, rows, :]
            fwd = d2 * fwd + w2 * at(src, i)
            adj = d1 * (adj + at(seed, i))
        payload[1, :, 0:expand] = adj
        payload[1, :, expand : 2 * expand] = fwd
        lane = lax.broadcasted_iota(jnp.int32, (lines, PAD), 1)
        sums = [jnp.sum(s, axis=1, keepdims=True) for s in steps]
        for way in (0, 1):
            payload[way, :, 2 * expand :] = jnp.where(lane < PAD // 2, sums[0], sums[1])
        mine = lax.axis_index(name)
        for k, out in enumerate(sent[axis], 1):
            out[...] = payload[((mine ^ k) < mine).astype(jnp.int32)]


def local_body(px, ct, rt, ss, mixed, back, s_loc, g_loc, pre, suf, m_in, m_gate, gated, x_t, c_t, src, seed):
    height, breadth, channels = px.shape
    expand = src.shape[0] * 128
    count = height * breadth
    inner, gate = mixed[:, :expand], mixed[:, expand:]
    s_in = sigmoid(inner)
    m_in[...] = s_in * (1.0 + inner * (1.0 - s_in))
    s_gate = sigmoid(gate)
    gate_silu = gate * s_gate
    gated[...] = gate_silu
    put(src, slice(None), inner * s_in)
    put(seed, slice(None), back[...] * gate_silu)
    m_gate[...] = back[...] * (s_gate * (1.0 + gate * (1.0 - s_gate)))
    x_t[...] = jnp.transpose(px[...].reshape(count, channels).astype(F32)).astype(BF16)
    c_t[...] = jnp.transpose(ct[...].reshape(count, channels).astype(F32)).astype(BF16)
    for axis in (0, 1):
        one, two = 2 * axis, 2 * axis + 1
        length = breadth if axis == 0 else height
        lines = height if axis == 0 else breadth

        def where(i):
            if axis == 0:
                return pl.ds(i, lines, stride=length)
            return pl.ds(i * lines, lines)

        steps = {d: ss[d] if axis == 0 else jnp.transpose(ss[d]) for d in (one, two)}

        def go(order, a, b, first):
            state = jnp.zeros((lines, expand), F32)
            carried = jnp.zeros((lines, expand), F32)
            upto = jnp.ones((lines, expand), F32)
            after = jnp.ones((lines, expand), F32)
            for i in order:
                da, wa = decay_pair(rt[a : a + 1, :], steps[a][:, i : i + 1])
                db, wb = decay_pair(rt[b : b + 1, :], steps[b][:, i : i + 1])
                state = da * state + wa * get(src, where(i))
                upto = upto * da
                adjoint = get(seed, where(i)) + carried
                carried = db * adjoint
                put(pre.at[a], where(i), upto)
                put(suf.at[b], where(i), wb * after)
                after = after * db
                grad = wb * adjoint
                if not first:
                    state_sum, grad = get(s_loc, where(i)) + state, get(g_loc, where(i)) + grad
                else:
                    state_sum = state
                put(s_loc, where(i), state_sum)
                put(g_loc, where(i), grad)

        go(range(length), one, two, axis == 0)
        go(reversed(range(length)), two, one, False)


def entering(axis, rates, parts):
    count, mine = len(parts) + 1, lax.axis_index(axis)
    expand = rates[0].shape[1]
    lines = parts[0].shape[0]
    sums = [
        jnp.concatenate([jnp.broadcast_to(part[:, c : c + 1], (lines, expand)) for c in (2 * expand, 2 * expand + PAD // 2)], axis=1)
        for part in parts
    ]
    both = jnp.concatenate(rates, axis=1)
    below = jnp.zeros((lines, 2 * expand), F32)
    above = jnp.zeros((lines, 2 * expand), F32)
    for k in range(1, count):
        place = mine ^ k
        between = jnp.zeros((lines, 2 * expand), F32)
        for m in range(1, count):
            if m == k:
                continue
            middle = mine ^ m
            inside = ((middle - mine) * (middle - place) < 0).astype(F32)
            between = between + inside * sums[m - 1]
        value = jnp.exp(-both * between) * parts[k - 1][:, : 2 * expand]
        lower = (place < mine).astype(F32)
        below = below + lower * value
        above = above + (1.0 - lower) * value
    return below, above


def join_body(shape, split, counts, rt, *refs):
    height, breadth = shape
    n_cols, n_rows = counts[0] - 1, counts[1] - 1
    from_cols, from_rows = refs[:n_cols], refs[n_cols : n_cols + n_rows]
    s_loc, g_loc, pre, suf, m_in, m_gate, gated, x_t, c_t, mix = refs[n_cols + n_rows : n_cols + n_rows + 10]
    outs = refs[n_cols + n_rows + 10 :]
    expand = s_loc.shape[0] * 128
    out_state = outs[-1]
    grads = outs[:-1]
    rates = [rt[d : d + 1, :] for d in range(4)]
    below, above = entering("rows", rates[2:], [r[...] for r in from_rows])
    f2, a3, a2, f3 = below[:, :expand], below[:, expand:], above[:, :expand], above[:, expand:]
    below, above = entering("cols", rates[:2], [r[...] for r in from_cols])
    for h in range(height):
        rows = slice(h * breadth, (h + 1) * breadth)
        f0, a1 = below[h : h + 1, :expand], below[h : h + 1, expand:]
        a0, f1 = above[h : h + 1, :expand], above[h : h + 1, expand:]
        total, grad = get(s_loc, rows), get(g_loc, rows)
        for d, (state_in, adjoint_in) in enumerate(((f0, a0), (f1, a1), (f2, a2), (f3, a3))):
            total = total + get(pre.at[d], rows) * state_in
            grad = grad + get(suf.at[d], rows) * adjoint_in
        out_state[rows, :] = (total * gated[rows, :]).astype(BF16)
        mix[rows, :expand] = (grad * m_in[rows, :]).astype(BF16)
        mix[rows, expand:] = (total * m_gate[rows, :]).astype(BF16)
    grad_in = jnp.dot(x_t[...], mix[...], preferred_element_type=F32)
    grad_out = jnp.dot(c_t[...], out_state[...], preferred_element_type=F32)
    if not split:
        grads[0][...] = grad_in
        grads[1][...] = grad_out
        return
    packed = grads[0]
    lane = lax.broadcasted_iota(jnp.int32, (16, 128), 1)
    for c in range(4):
        for t in range(2):
            top = grad_out[32 * c : 32 * c + 16, 128 * t : 128 * t + 128]
            bottom = grad_out[32 * c + 16 : 32 * c + 32, 128 * t : 128 * t + 128]
            low = jnp.where(lane < 64, top, pltpu.roll(bottom, 64, 1))
            high = jnp.where(lane < 64, pltpu.roll(top, 64, 1), bottom)
            for k, piece in ((0, low), (1, high)):
                r = 2 * t + k
                packed[c & 1, c >> 1, k, t, 0:32, :] = grad_in[32 * r : 32 * r + 32, 128 * c : 128 * c + 128]
                packed[c & 1, c >> 1, k, t, 32:48, :] = piece


def pixels_body(ct, mix, wi, out):
    height, breadth, channels = ct.shape
    grad = lax.dot_general(mix[...], wi[...], contract_cols, preferred_element_type=F32)
    cot = ct[...].reshape(height * breadth, channels).astype(F32)
    out[...] = (cot + grad).astype(BF16).reshape(height, breadth, channels)


def final_body(mine, other, g_in, g_out):
    total = mine[...] + other[...]
    g_in[...] = total[0:32, :]
    g_out[0:16, :] = total[32:48, 0:64]
    g_out[16:32, :] = total[32:48, 64:128]


def partner(value, axis, bit):
    return lax.ppermute(value, axis, [(i, i ^ bit) for i in range(lax.axis_size(axis))])


def exchange(payloads, axis):
    return [partner(payload, axis, k) for k, payload in enumerate(payloads, 1)]


def halve(value, axis, bit):
    mine = (lax.axis_index(axis) & bit) // bit
    pick = lambda i: lax.dynamic_index_in_dim(value, i, 0, keepdims=False)
    return pick(mine), partner(pick(1 - mine), axis, bit)


def per_device(pixels, cotangent, w_in, w_out, decay_rates, step_sizes):
    height, breadth, channels = pixels.shape
    expand = w_out.shape[0]
    count = height * breadth
    rows, cols = lax.axis_size("rows"), lax.axis_size("cols")
    full = jax.ShapeDtypeStruct((count, expand), F32)
    tall = jax.ShapeDtypeStruct((expand // 128, count, 128), F32)
    four_tall = jax.ShapeDtypeStruct((4, expand // 128, count, 128), F32)
    four = jax.ShapeDtypeStruct((4, count, expand), F32)
    wide = jax.ShapeDtypeStruct((count, 2 * expand), F32)
    like = lambda a: jax.ShapeDtypeStruct(a.shape, a.dtype)
    pay_cols = jax.ShapeDtypeStruct((height, 2 * expand + PAD), F32)
    pay_rows = jax.ShapeDtypeStruct((breadth, 2 * expand + PAD), F32)
    pays = (pay_cols,) * (cols - 1) + (pay_rows,) * (rows - 1)
    outs = vmem_call(
        functools.partial(edges_body, (cols, rows)),
        (*pays, like(pixels), like(cotangent), like(w_in), like(decay_rates), like(step_sizes), wide, full),
        scratch=[
            *(pltpu.VMEM(s.shape, F32) for s in (tall, tall, four, four)),
            pltpu.VMEM(w_out.shape, BF16),
            pltpu.VMEM((2, 2, *pay_cols.shape), F32),
            pltpu.SemaphoreType.DMA((6,)),
        ],
        given=pltpu.HBM,
    )(pixels, cotangent, w_in, w_out, decay_rates, step_sizes)
    sent = outs[: len(pays)]
    px, ct, wi, rt, ss, mixed, back = outs[len(pays) :]
    turned = jax.ShapeDtypeStruct((channels, count), BF16)
    s_loc, g_loc, pre, suf, m_in, m_gate, gated, x_t, c_t = vmem_call(
        local_body,
        (tall, tall, four_tall, four_tall, full, full, full, turned, turned),
        scratch=[pltpu.VMEM(tall.shape, F32)] * 2,
    )(px, ct, rt, ss, mixed, back)
    from_rows = exchange(sent[cols - 1 :], "rows")
    from_cols = exchange(sent[: cols - 1], "cols")
    split = rows == 4 and cols == 4 and channels == 128 and expand == 256
    if split:
        grads = (jax.ShapeDtypeStruct((2, 2, 2, 2, 48, 128), F32),)
    else:
        grads = (
            jax.ShapeDtypeStruct((channels, 2 * expand), F32),
            jax.ShapeDtypeStruct((channels, expand), F32),
        )
    outs = vmem_call(
        functools.partial(join_body, (height, breadth), split, (cols, rows)),
        (jax.ShapeDtypeStruct((count, 2 * expand), BF16), *grads, jax.ShapeDtypeStruct((count, expand), BF16)),
    )(rt, *from_cols, *from_rows, s_loc, g_loc, pre, suf, m_in, m_gate, gated, x_t, c_t)
    mix, grads = outs[0], outs[1:-1]
    grad_pixels = vmem_call(pixels_body, like(pixels), kept=False)(ct, mix, wi)
    if split:
        value = grads[0]
        for axis, bit in (("cols", 1), ("cols", 2), ("rows", 1)):
            kept, got = halve(value, axis, bit)
            value = kept + got
        kept, got = halve(value, "rows", 2)
        grad_in, grad_out = vmem_call(
            final_body, (jax.ShapeDtypeStruct((32, 128), F32), jax.ShapeDtypeStruct((32, 64), F32)), kept=False
        )(kept, got)
        return grad_pixels, grad_in, jnp.transpose(grad_out)
    full_in, full_out = grads[0], jnp.transpose(grads[1])
    full_in = lax.psum_scatter(full_in, "cols", scatter_dimension=1, tiled=True)
    full_out = lax.psum_scatter(full_out, "cols", scatter_dimension=1, tiled=True)
    return (
        grad_pixels,
        lax.psum_scatter(full_in, "rows", scatter_dimension=0, tiled=True),
        lax.psum_scatter(full_out, "rows", scatter_dimension=0, tiled=True),
    )


def solution(mesh):
    return jax.shard_map(
        per_device,
        mesh=mesh,
        in_specs=(
            P(("groups", "rows"), "cols", None),
            P(("groups", "rows"), "cols", None),
            P(),
            P(),
            P(),
            P(None, ("groups", "rows"), "cols"),
        ),
        out_specs=(
            P(("groups", "rows"), "cols", None),
            P(("groups", "rows"), "cols"),
            P(("groups", "rows"), "cols"),
        ),
        check_vma=False,
    )
```

```python
import functools

import jax
import jax.numpy as jnp
from jax import lax
from jax.experimental import pallas as pl
from jax.experimental.pallas import tpu as pltpu
from jax.sharding import PartitionSpec as P

F32 = jnp.float32
BF16 = jnp.bfloat16
contract_rows = (((0,), (0,)), ((), ()))
contract_cols = (((1,), (1,)), ((), ()))
VMEM_LIMIT = 6 * 1024 * 1024
PAD = 128


def vmem_call(body, out_shape, scratch=(), given=pltpu.VMEM, kept=True):
    spec = pl.BlockSpec(memory_space=pltpu.VMEM)
    if kept:
        out_shape = jax.tree.map(lambda s: pltpu.VMEM(s.shape, s.dtype), out_shape)

    def call(*operands):
        operands = [pltpu.with_memory_space_constraint(a, given) for a in operands]
        return pl.pallas_call(
            body,
            out_shape=out_shape,
            in_specs=[pl.BlockSpec(memory_space=given)] * len(operands),
            out_specs=jax.tree.map(lambda _: spec, out_shape),
            scratch_shapes=scratch,
            compiler_params=pltpu.CompilerParams(vmem_limit_bytes=VMEM_LIMIT),
            cost_estimate=pl.CostEstimate(flops=0, bytes_accessed=0, transcendentals=0),
        )(*operands)

    return call


def get(ref, rows):
    return jnp.concatenate([ref[k, rows, :] for k in range(ref.shape[0])], axis=1)


def put(ref, rows, value):
    for k in range(ref.shape[0]):
        ref[k, rows, :] = value[:, 128 * k : 128 * k + 128]


def sigmoid(value):
    return 1.0 / (1.0 + jnp.exp(-value))


def decay_pair(rate, step):
    decay = jnp.exp(-(rate * step))
    rest = 1.0 - decay * decay
    return decay, rest * lax.rsqrt(rest)


def edges_body(order, px_in, ct_in, wi_in, wo_in, rt_in, ss_in, *refs):
    sent = refs[: len(order)]
    px, ct, wi, rt, ss, mixed, back, src, seed, dec, wgt, wo, ways, sems = refs[len(order) :]
    pairs = ((px_in, px), (wi_in, wi), (ct_in, ct), (wo_in, wo), (ss_in, ss), (rt_in, rt))
    copies = [pltpu.make_async_copy(a, b, sems.at[k]) for k, (a, b) in enumerate(pairs)]
    for copy in copies:
        copy.start()
    height, breadth, channels = px.shape
    expand = wo.shape[0]
    count = height * breadth
    copies[0].wait()
    copies[1].wait()
    both = jnp.dot(px[...].reshape(count, channels), wi[...], preferred_element_type=F32)
    mixed[...] = both
    copies[2].wait()
    copies[3].wait()
    cot = ct[...].reshape(count, channels)
    bg = lax.dot_general(cot, wo[...], contract_cols, preferred_element_type=F32)
    back[...] = bg
    inner, gate = both[:, :expand], both[:, expand:]
    put(src, slice(None), inner * sigmoid(inner))
    put(seed, slice(None), bg * (gate * sigmoid(gate)))
    copies[4].wait()
    copies[5].wait()

    for axis, name in ((0, "cols"), (1, "rows")):
        payload = ways.at[axis]
        one, two = 2 * axis, 2 * axis + 1
        length = breadth if axis == 0 else height
        lines = height if axis == 0 else breadth

        def at(ref, i):
            return get(ref, pl.ds(i, lines, stride=length) if axis == 0 else pl.ds(i * lines, lines))

        steps = [ss[d] if axis == 0 else jnp.transpose(ss[d]) for d in (one, two)]
        rates = [rt[d : d + 1, :] for d in (one, two)]
        fwd = jnp.zeros((lines, expand), F32)
        adj = jnp.zeros((lines, expand), F32)
        for i in range(length):
            rows = slice(i * lines, (i + 1) * lines)
            d1, w1 = decay_pair(rates[0], steps[0][:, i : i + 1])
            d2, w2 = decay_pair(rates[1], steps[1][:, i : i + 1])
            dec[one, rows, :] = d1
            wgt[one, rows, :] = w1
            dec[two, rows, :] = d2
            wgt[two, rows, :] = w2
            fwd = d1 * fwd + w1 * at(src, i)
            adj = d2 * (adj + at(seed, i))
        payload[0, :, 0:expand] = fwd
        payload[0, :, expand : 2 * expand] = adj
        fwd = jnp.zeros((lines, expand), F32)
        adj = jnp.zeros((lines, expand), F32)
        for i in reversed(range(length)):
            rows = slice(i * lines, (i + 1) * lines)
            d1, d2, w2 = dec[one, rows, :], dec[two, rows, :], wgt[two, rows, :]
            fwd = d2 * fwd + w2 * at(src, i)
            adj = d1 * (adj + at(seed, i))
        payload[1, :, 0:expand] = adj
        payload[1, :, expand : 2 * expand] = fwd
        lane = lax.broadcasted_iota(jnp.int32, (lines, PAD), 1)
        sums = [jnp.sum(s, axis=1, keepdims=True) for s in steps]
        for way in (0, 1):
            payload[way, :, 2 * expand :] = jnp.where(lane < PAD // 2, sums[0], sums[1])
        mine = lax.axis_index(name)
        for (out_axis, k), out in zip(order, sent):
            if out_axis == name:
                out[...] = payload[((mine ^ k) < mine).astype(jnp.int32)]


def local_body(px, ct, rt, ss, mixed, back, s_loc, g_loc, pre, suf, m_in, m_gate, gated, x_t, c_t, src, seed):
    height, breadth, channels = px.shape
    expand = src.shape[0] * 128
    count = height * breadth
    inner, gate = mixed[:, :expand], mixed[:, expand:]
    s_in = sigmoid(inner)
    m_in[...] = s_in * (1.0 + inner * (1.0 - s_in))
    s_gate = sigmoid(gate)
    gate_silu = gate * s_gate
    gated[...] = gate_silu
    put(src, slice(None), inner * s_in)
    put(seed, slice(None), back[...] * gate_silu)
    m_gate[...] = back[...] * (s_gate * (1.0 + gate * (1.0 - s_gate)))
    x_t[...] = jnp.transpose(px[...].reshape(count, channels).astype(F32)).astype(BF16)
    c_t[...] = jnp.transpose(ct[...].reshape(count, channels).astype(F32)).astype(BF16)
    for axis in (0, 1):
        one, two = 2 * axis, 2 * axis + 1
        length = breadth if axis == 0 else height
        lines = height if axis == 0 else breadth

        def where(i):
            if axis == 0:
                return pl.ds(i, lines, stride=length)
            return pl.ds(i * lines, lines)

        steps = {d: ss[d] if axis == 0 else jnp.transpose(ss[d]) for d in (one, two)}

        def go(order, a, b, first):
            state = jnp.zeros((lines, expand), F32)
            carried = jnp.zeros((lines, expand), F32)
            upto = jnp.ones((lines, expand), F32)
            after = jnp.ones((lines, expand), F32)
            for i in order:
                da, wa = decay_pair(rt[a : a + 1, :], steps[a][:, i : i + 1])
                db, wb = decay_pair(rt[b : b + 1, :], steps[b][:, i : i + 1])
                state = da * state + wa * get(src, where(i))
                upto = upto * da
                adjoint = get(seed, where(i)) + carried
                carried = db * adjoint
                put(pre.at[a], where(i), upto)
                put(suf.at[b], where(i), wb * after)
                after = after * db
                grad = wb * adjoint
                if not first:
                    state_sum, grad = get(s_loc, where(i)) + state, get(g_loc, where(i)) + grad
                else:
                    state_sum = state
                put(s_loc, where(i), state_sum)
                put(g_loc, where(i), grad)

        go(range(length), one, two, axis == 0)
        go(reversed(range(length)), two, one, False)


def entering(axis, rates, received):
    parts = [received[key] for key in sorted(received) if key[0] == axis]
    count, mine = len(parts) + 1, lax.axis_index(axis)
    expand = rates[0].shape[1]
    lines = parts[0].shape[0]
    sums = [
        jnp.concatenate([jnp.broadcast_to(part[:, c : c + 1], (lines, expand)) for c in (2 * expand, 2 * expand + PAD // 2)], axis=1)
        for part in parts
    ]
    both = jnp.concatenate(rates, axis=1)
    below = jnp.zeros((lines, 2 * expand), F32)
    above = jnp.zeros((lines, 2 * expand), F32)
    for k in range(1, count):
        place = mine ^ k
        between = jnp.zeros((lines, 2 * expand), F32)
        for m in range(1, count):
            if m == k:
                continue
            middle = mine ^ m
            inside = ((middle - mine) * (middle - place) < 0).astype(F32)
            between = between + inside * sums[m - 1]
        value = jnp.exp(-both * between) * parts[k - 1][:, : 2 * expand]
        lower = (place < mine).astype(F32)
        below = below + lower * value
        above = above + (1.0 - lower) * value
    return below, above


def join_body(shape, split, order, rt, *refs):
    height, breadth = shape
    received = {key: ref[...] for key, ref in zip(order, refs)}
    s_loc, g_loc, pre, suf, m_in, m_gate, gated, x_t, c_t, mix = refs[len(order) : len(order) + 10]
    outs = refs[len(order) + 10 :]
    expand = s_loc.shape[0] * 128
    out_state = outs[-1]
    grads = outs[:-1]
    rates = [rt[d : d + 1, :] for d in range(4)]
    below, above = entering("rows", rates[2:], received)
    f2, a3, a2, f3 = below[:, :expand], below[:, expand:], above[:, :expand], above[:, expand:]
    below, above = entering("cols", rates[:2], received)
    for h in range(height):
        rows = slice(h * breadth, (h + 1) * breadth)
        f0, a1 = below[h : h + 1, :expand], below[h : h + 1, expand:]
        a0, f1 = above[h : h + 1, :expand], above[h : h + 1, expand:]
        total, grad = get(s_loc, rows), get(g_loc, rows)
        for d, (state_in, adjoint_in) in enumerate(((f0, a0), (f1, a1), (f2, a2), (f3, a3))):
            total = total + get(pre.at[d], rows) * state_in
            grad = grad + get(suf.at[d], rows) * adjoint_in
        out_state[rows, :] = (total * gated[rows, :]).astype(BF16)
        mix[rows, :expand] = (grad * m_in[rows, :]).astype(BF16)
        mix[rows, expand:] = (total * m_gate[rows, :]).astype(BF16)
    grad_in = jnp.dot(x_t[...], mix[...], preferred_element_type=F32)
    grad_out = jnp.dot(c_t[...], out_state[...], preferred_element_type=F32)
    if not split:
        grads[0][...] = grad_in
        grads[1][...] = grad_out
        return
    packed = grads[0]
    lane = lax.broadcasted_iota(jnp.int32, (16, 128), 1)
    for c in range(4):
        for t in range(2):
            top = grad_out[32 * c : 32 * c + 16, 128 * t : 128 * t + 128]
            bottom = grad_out[32 * c + 16 : 32 * c + 32, 128 * t : 128 * t + 128]
            low = jnp.where(lane < 64, top, pltpu.roll(bottom, 64, 1))
            high = jnp.where(lane < 64, pltpu.roll(top, 64, 1), bottom)
            for k, piece in ((0, low), (1, high)):
                r = 2 * t + k
                packed[c & 1, c >> 1, k, t, 0:32, :] = grad_in[32 * r : 32 * r + 32, 128 * c : 128 * c + 128]
                packed[c & 1, c >> 1, k, t, 32:48, :] = piece


def pixels_body(ct, mix, wi, out):
    height, breadth, channels = ct.shape
    grad = lax.dot_general(mix[...], wi[...], contract_cols, preferred_element_type=F32)
    cot = ct[...].reshape(height * breadth, channels).astype(F32)
    out[...] = (cot + grad).astype(BF16).reshape(height, breadth, channels)


def final_body(mine, other, g_in, g_out):
    total = mine[...] + other[...]
    g_in[...] = total[0:32, :]
    g_out[0:16, :] = total[32:48, 0:64]
    g_out[16:32, :] = total[32:48, 64:128]


def partner(value, axis, bit):
    return lax.ppermute(value, axis, [(i, i ^ bit) for i in range(lax.axis_size(axis))])


def send_order(cols, rows):
    return [("rows", k) for k in reversed(range(1, rows))] + [("cols", k) for k in reversed(range(1, cols))]


def halve(value, axis, bit):
    mine = (lax.axis_index(axis) & bit) // bit
    pick = lambda i: lax.dynamic_index_in_dim(value, i, 0, keepdims=False)
    return pick(mine), partner(pick(1 - mine), axis, bit)


def per_device(pixels, cotangent, w_in, w_out, decay_rates, step_sizes):
    height, breadth, channels = pixels.shape
    expand = w_out.shape[0]
    count = height * breadth
    rows, cols = lax.axis_size("rows"), lax.axis_size("cols")
    full = jax.ShapeDtypeStruct((count, expand), F32)
    tall = jax.ShapeDtypeStruct((expand // 128, count, 128), F32)
    four_tall = jax.ShapeDtypeStruct((4, expand // 128, count, 128), F32)
    four = jax.ShapeDtypeStruct((4, count, expand), F32)
    wide = jax.ShapeDtypeStruct((count, 2 * expand), F32)
    like = lambda a: jax.ShapeDtypeStruct(a.shape, a.dtype)
    pay_cols = jax.ShapeDtypeStruct((height, 2 * expand + PAD), F32)
    pay_rows = jax.ShapeDtypeStruct((breadth, 2 * expand + PAD), F32)
    order = send_order(cols, rows)
    pays = tuple(pay_cols if axis == "cols" else pay_rows for axis, _ in order)
    outs = vmem_call(
        functools.partial(edges_body, order),
        (*pays, like(pixels), like(cotangent), like(w_in), like(decay_rates), like(step_sizes), wide, full),
        scratch=[
            *(pltpu.VMEM(s.shape, F32) for s in (tall, tall, four, four)),
            pltpu.VMEM(w_out.shape, BF16),
            pltpu.VMEM((2, 2, *pay_cols.shape), F32),
            pltpu.SemaphoreType.DMA((6,)),
        ],
        given=pltpu.HBM,
    )(pixels, cotangent, w_in, w_out, decay_rates, step_sizes)
    sent = outs[: len(pays)]
    px, ct, wi, rt, ss, mixed, back = outs[len(pays) :]
    turned = jax.ShapeDtypeStruct((channels, count), BF16)
    s_loc, g_loc, pre, suf, m_in, m_gate, gated, x_t, c_t = vmem_call(
        local_body,
        (tall, tall, four_tall, four_tall, full, full, full, turned, turned),
        scratch=[pltpu.VMEM(tall.shape, F32)] * 2,
    )(px, ct, rt, ss, mixed, back)
    received = {key: partner(payload, *key) for key, payload in zip(order, sent)}
    split = rows == 4 and cols == 4 and channels == 128 and expand == 256
    if split:
        grads = (jax.ShapeDtypeStruct((2, 2, 2, 2, 48, 128), F32),)
    else:
        grads = (
            jax.ShapeDtypeStruct((channels, 2 * expand), F32),
            jax.ShapeDtypeStruct((channels, expand), F32),
        )
    outs = vmem_call(
        functools.partial(join_body, (height, breadth), split, order),
        (jax.ShapeDtypeStruct((count, 2 * expand), BF16), *grads, jax.ShapeDtypeStruct((count, expand), BF16)),
    )(rt, *received.values(), s_loc, g_loc, pre, suf, m_in, m_gate, gated, x_t, c_t)
    mix, grads = outs[0], outs[1:-1]
    grad_pixels = vmem_call(pixels_body, like(pixels), kept=False)(ct, mix, wi)
    if split:
        value = grads[0]
        for axis, bit in (("cols", 1), ("cols", 2), ("rows", 1)):
            kept, got = halve(value, axis, bit)
            value = kept + got
        kept, got = halve(value, "rows", 2)
        grad_in, grad_out = vmem_call(
            final_body, (jax.ShapeDtypeStruct((32, 128), F32), jax.ShapeDtypeStruct((32, 64), F32)), kept=False
        )(kept, got)
        return grad_pixels, grad_in, jnp.transpose(grad_out)
    full_in, full_out = grads[0], jnp.transpose(grads[1])
    full_in = lax.psum_scatter(full_in, "cols", scatter_dimension=1, tiled=True)
    full_out = lax.psum_scatter(full_out, "cols", scatter_dimension=1, tiled=True)
    return (
        grad_pixels,
        lax.psum_scatter(full_in, "rows", scatter_dimension=0, tiled=True),
        lax.psum_scatter(full_out, "rows", scatter_dimension=0, tiled=True),
    )


def solution(mesh):
    return jax.shard_map(
        per_device,
        mesh=mesh,
        in_specs=(
            P(("groups", "rows"), "cols", None),
            P(("groups", "rows"), "cols", None),
            P(),
            P(),
            P(),
            P(None, ("groups", "rows"), "cols"),
        ),
        out_specs=(
            P(("groups", "rows"), "cols", None),
            P(("groups", "rows"), "cols"),
            P(("groups", "rows"), "cols"),
        ),
        check_vma=False,
    )
```

```python
import functools

import jax
import jax.numpy as jnp
from jax import lax
from jax.experimental import pallas as pl
from jax.experimental.pallas import tpu as pltpu
from jax.sharding import PartitionSpec as P

F32 = jnp.float32
BF16 = jnp.bfloat16
contract_rows = (((0,), (0,)), ((), ()))
contract_cols = (((1,), (1,)), ((), ()))
VMEM_LIMIT = 6 * 1024 * 1024
PAD = 128


def vmem_call(body, out_shape, scratch=(), given=pltpu.VMEM, kept=True):
    spec = pl.BlockSpec(memory_space=pltpu.VMEM)
    if kept:
        out_shape = jax.tree.map(lambda s: pltpu.VMEM(s.shape, s.dtype), out_shape)

    def call(*operands):
        operands = [pltpu.with_memory_space_constraint(a, given) for a in operands]
        return pl.pallas_call(
            body,
            out_shape=out_shape,
            in_specs=[pl.BlockSpec(memory_space=given)] * len(operands),
            out_specs=jax.tree.map(lambda _: spec, out_shape),
            scratch_shapes=scratch,
            compiler_params=pltpu.CompilerParams(vmem_limit_bytes=VMEM_LIMIT),
            cost_estimate=pl.CostEstimate(flops=0, bytes_accessed=0, transcendentals=0),
        )(*operands)

    return call


def get(ref, rows):
    return jnp.concatenate([ref[k, rows, :] for k in range(ref.shape[0])], axis=1)


def put(ref, rows, value):
    for k in range(ref.shape[0]):
        ref[k, rows, :] = value[:, 128 * k : 128 * k + 128]


def sigmoid(value):
    return 0.5 * jnp.tanh(0.5 * value) + 0.5


def decay_pair(rate, step):
    decay = jnp.exp(-(rate * step))
    rest = 1.0 - decay * decay
    return decay, rest * lax.rsqrt(rest)


def edges_body(order, px_in, ct_in, wi_in, wo_in, rt_in, ss_in, *refs):
    sent = refs[: len(order)]
    px, ct, rt, mixed, back, dec, wgt, wi, wo, ss, src, seed, ways, sems = refs[len(order) :]
    pairs = ((px_in, px), (wi_in, wi), (ct_in, ct), (wo_in, wo), (ss_in, ss), (rt_in, rt))
    copies = [pltpu.make_async_copy(a, b, sems.at[k]) for k, (a, b) in enumerate(pairs)]
    for copy in copies:
        copy.start()
    height, breadth, channels = px.shape
    expand = wo.shape[0]
    count = height * breadth
    copies[0].wait()
    copies[1].wait()
    both = jnp.dot(px[...].reshape(count, channels), wi[...], preferred_element_type=F32)
    mixed[...] = both
    inner, gate = both[:, :expand], both[:, expand:]
    put(src, slice(None), inner * sigmoid(inner))
    copies[2].wait()
    copies[3].wait()
    cot = ct[...].reshape(count, channels)
    bg = lax.dot_general(cot, wo[...], contract_cols, preferred_element_type=F32)
    back[...] = bg
    put(seed, slice(None), bg * (gate * sigmoid(gate)))
    copies[4].wait()
    copies[5].wait()

    for axis, name in ((0, "cols"), (1, "rows")):
        payload = ways.at[axis]
        one, two = 2 * axis, 2 * axis + 1
        length = breadth if axis == 0 else height
        lines = height if axis == 0 else breadth

        def at(ref, i):
            return get(ref, pl.ds(i, lines, stride=length) if axis == 0 else pl.ds(i * lines, lines))

        steps = [ss[d] if axis == 0 else jnp.transpose(ss[d]) for d in (one, two)]
        rates = [rt[d : d + 1, :] for d in (one, two)]
        fwd = jnp.zeros((lines, expand), F32)
        adj = jnp.zeros((lines, expand), F32)
        for i in range(length):
            rows = slice(i * lines, (i + 1) * lines)
            d1, w1 = decay_pair(rates[0], steps[0][:, i : i + 1])
            d2, w2 = decay_pair(rates[1], steps[1][:, i : i + 1])
            dec[one, rows, :] = d1
            wgt[one, rows, :] = w1
            dec[two, rows, :] = d2
            wgt[two, rows, :] = w2
            fwd = d1 * fwd + w1 * at(src, i)
            adj = d2 * (adj + at(seed, i))
        payload[0, :, 0:expand] = fwd
        payload[0, :, expand : 2 * expand] = adj
        fwd = jnp.zeros((lines, expand), F32)
        adj = jnp.zeros((lines, expand), F32)
        for i in reversed(range(length)):
            rows = slice(i * lines, (i + 1) * lines)
            d1, d2, w2 = dec[one, rows, :], dec[two, rows, :], wgt[two, rows, :]
            fwd = d2 * fwd + w2 * at(src, i)
            adj = d1 * (adj + at(seed, i))
        payload[1, :, 0:expand] = adj
        payload[1, :, expand : 2 * expand] = fwd
        lane = lax.broadcasted_iota(jnp.int32, (lines, PAD), 1)
        sums = [jnp.sum(s, axis=1, keepdims=True) for s in steps]
        for way in (0, 1):
            payload[way, :, 2 * expand :] = jnp.where(lane < PAD // 2, sums[0], sums[1])
        mine = lax.axis_index(name)
        for (out_axis, k), out in zip(order, sent):
            if out_axis == name:
                out[...] = payload[((mine ^ k) < mine).astype(jnp.int32)]


def local_body(px, ct, mixed, back, dec, wgt, s_loc, g_loc, pre, suf, m_in, m_gate, gated, x_t, c_t, src, seed):
    height, breadth, channels = px.shape
    expand = src.shape[0] * 128
    count = height * breadth
    inner, gate = mixed[:, :expand], mixed[:, expand:]
    s_in, s_gate = sigmoid(inner), sigmoid(gate)
    gate_silu = gate * s_gate
    put(src, slice(None), inner * s_in)
    put(seed, slice(None), back[...] * gate_silu)
    m_in[...] = s_in * (1.0 + inner * (1.0 - s_in))
    gated[...] = gate_silu
    m_gate[...] = back[...] * (s_gate * (1.0 + gate * (1.0 - s_gate)))
    x_t[...] = jnp.transpose(px[...].reshape(count, channels).astype(F32)).astype(BF16)
    c_t[...] = jnp.transpose(ct[...].reshape(count, channels).astype(F32)).astype(BF16)
    for axis in (0, 1):
        one, two = 2 * axis, 2 * axis + 1
        length = breadth if axis == 0 else height
        lines = height if axis == 0 else breadth

        def where(i):
            if axis == 0:
                return pl.ds(i, lines, stride=length)
            return pl.ds(i * lines, lines)

        def go(order, a, b, first):
            state = jnp.zeros((lines, expand), F32)
            carried = jnp.zeros((lines, expand), F32)
            upto = jnp.ones((lines, expand), F32)
            after = jnp.ones((lines, expand), F32)
            for i in order:
                rows = slice(i * lines, (i + 1) * lines)
                da, wa, db, wb = dec[a, rows, :], wgt[a, rows, :], dec[b, rows, :], wgt[b, rows, :]
                state = da * state + wa * get(src, where(i))
                upto = upto * da
                adjoint = get(seed, where(i)) + carried
                carried = db * adjoint
                put(pre.at[a], where(i), upto)
                put(suf.at[b], where(i), wb * after)
                after = after * db
                grad = wb * adjoint
                if not first:
                    state_sum, grad = get(s_loc, where(i)) + state, get(g_loc, where(i)) + grad
                else:
                    state_sum = state
                put(s_loc, where(i), state_sum)
                put(g_loc, where(i), grad)

        go(range(length), one, two, axis == 0)
        go(reversed(range(length)), two, one, False)


def entering(axis, rates, received):
    parts = [received[key] for key in sorted(received) if key[0] == axis]
    count, mine = len(parts) + 1, lax.axis_index(axis)
    expand = rates[0].shape[1]
    lines = parts[0].shape[0]
    sums = [
        jnp.concatenate([jnp.broadcast_to(part[:, c : c + 1], (lines, expand)) for c in (2 * expand, 2 * expand + PAD // 2)], axis=1)
        for part in parts
    ]
    both = jnp.concatenate(rates, axis=1)
    below = jnp.zeros((lines, 2 * expand), F32)
    above = jnp.zeros((lines, 2 * expand), F32)
    for k in range(1, count):
        place = mine ^ k
        between = jnp.zeros((lines, 2 * expand), F32)
        for m in range(1, count):
            if m == k:
                continue
            middle = mine ^ m
            inside = ((middle - mine) * (middle - place) < 0).astype(F32)
            between = between + inside * sums[m - 1]
        value = jnp.exp(-both * between) * parts[k - 1][:, : 2 * expand]
        lower = (place < mine).astype(F32)
        below = below + lower * value
        above = above + (1.0 - lower) * value
    return below, above


def join_body(shape, split, order, rt, *refs):
    height, breadth = shape
    received = {key: ref[...] for key, ref in zip(order, refs)}
    s_loc, g_loc, pre, suf, m_in, m_gate, gated, x_t, c_t, mix = refs[len(order) : len(order) + 10]
    outs = refs[len(order) + 10 :]
    expand = s_loc.shape[0] * 128
    out_state = outs[-1]
    grads = outs[:-1]
    rates = [rt[d : d + 1, :] for d in range(4)]
    below, above = entering("rows", rates[2:], received)
    f2, a3, a2, f3 = below[:, :expand], below[:, expand:], above[:, :expand], above[:, expand:]
    below, above = entering("cols", rates[:2], received)
    for h in range(height):
        rows = slice(h * breadth, (h + 1) * breadth)
        f0, a1 = below[h : h + 1, :expand], below[h : h + 1, expand:]
        a0, f1 = above[h : h + 1, :expand], above[h : h + 1, expand:]
        total, grad = get(s_loc, rows), get(g_loc, rows)
        for d, (state_in, adjoint_in) in enumerate(((f0, a0), (f1, a1), (f2, a2), (f3, a3))):
            total = total + get(pre.at[d], rows) * state_in
            grad = grad + get(suf.at[d], rows) * adjoint_in
        out_state[rows, :] = (total * gated[rows, :]).astype(BF16)
        mix[rows, :expand] = (grad * m_in[rows, :]).astype(BF16)
        mix[rows, expand:] = (total * m_gate[rows, :]).astype(BF16)
    grad_in = jnp.dot(x_t[...], mix[...], preferred_element_type=F32)
    grad_out = jnp.dot(c_t[...], out_state[...], preferred_element_type=F32)
    if not split:
        grads[0][...] = grad_in
        grads[1][...] = grad_out
        return
    packed = grads[0]
    lane = lax.broadcasted_iota(jnp.int32, (16, 128), 1)
    for c in range(4):
        for t in range(2):
            top = grad_out[32 * c : 32 * c + 16, 128 * t : 128 * t + 128]
            bottom = grad_out[32 * c + 16 : 32 * c + 32, 128 * t : 128 * t + 128]
            low = jnp.where(lane < 64, top, pltpu.roll(bottom, 64, 1))
            high = jnp.where(lane < 64, pltpu.roll(top, 64, 1), bottom)
            for k, piece in ((0, low), (1, high)):
                r = 2 * t + k
                packed[c, r, 0:32, :] = grad_in[32 * r : 32 * r + 32, 128 * c : 128 * c + 128]
                packed[c, r, 32:48, :] = piece


def pixels_body(ct, mix, wi, out):
    height, breadth, channels = ct.shape
    grad = lax.dot_general(mix[...], wi[...], contract_cols, preferred_element_type=F32)
    cot = ct[...].reshape(height * breadth, channels).astype(F32)
    out[...] = (cot + grad).astype(BF16).reshape(height, breadth, channels)


def final_body(mine, one, two, three, g_in, g_out):
    total = (mine[...] + one[...]) + (two[...] + three[...])
    g_in[...] = total[0:32, :]
    g_out[0:16, :] = total[32:48, 0:64]
    g_out[16:32, :] = total[32:48, 64:128]


def partner(value, axis, bit):
    return lax.ppermute(value, axis, [(i, i ^ bit) for i in range(lax.axis_size(axis))])


def send_order(cols, rows):
    return [("rows", k) for k in reversed(range(1, rows))] + [("cols", k) for k in reversed(range(1, cols))]


def shifted(value, axis, k):
    count = lax.axis_size(axis)
    return lax.ppermute(value, axis, [(i, (i + k) % count) for i in range(count)])


def spread(value, axis, order):
    count, mine = lax.axis_size(axis), lax.axis_index(axis)
    pick = lambda i: lax.dynamic_index_in_dim(value, i, 0, keepdims=False)
    return [pick(mine)] + [shifted(pick(lax.rem(mine + k, count)), axis, k) for k in order]


def per_device(pixels, cotangent, w_in, w_out, decay_rates, step_sizes):
    height, breadth, channels = pixels.shape
    expand = w_out.shape[0]
    count = height * breadth
    rows, cols = lax.axis_size("rows"), lax.axis_size("cols")
    full = jax.ShapeDtypeStruct((count, expand), F32)
    tall = jax.ShapeDtypeStruct((expand // 128, count, 128), F32)
    four_tall = jax.ShapeDtypeStruct((4, expand // 128, count, 128), F32)
    four = jax.ShapeDtypeStruct((4, count, expand), F32)
    wide = jax.ShapeDtypeStruct((count, 2 * expand), F32)
    like = lambda a: jax.ShapeDtypeStruct(a.shape, a.dtype)
    pay_cols = jax.ShapeDtypeStruct((height, 2 * expand + PAD), F32)
    pay_rows = jax.ShapeDtypeStruct((breadth, 2 * expand + PAD), F32)
    order = send_order(cols, rows)
    pays = tuple(pay_cols if axis == "cols" else pay_rows for axis, _ in order)
    outs = vmem_call(
        functools.partial(edges_body, order),
        (*pays, like(pixels), like(cotangent), like(decay_rates), wide, full, four, four),
        scratch=[
            pltpu.VMEM(w_in.shape, BF16),
            pltpu.VMEM(w_out.shape, BF16),
            pltpu.VMEM(step_sizes.shape, F32),
            pltpu.VMEM(tall.shape, F32),
            pltpu.VMEM(tall.shape, F32),
            pltpu.VMEM((2, 2, *pay_cols.shape), F32),
            pltpu.SemaphoreType.DMA((6,)),
        ],
        given=pltpu.HBM,
    )(pixels, cotangent, w_in, w_out, decay_rates, step_sizes)
    sent = outs[: len(pays)]
    px, ct, rt, mixed, back, dec, wgt = outs[len(pays) :]
    turned = jax.ShapeDtypeStruct((channels, count), BF16)
    s_loc, g_loc, pre, suf, m_in, m_gate, gated, x_t, c_t = vmem_call(
        local_body,
        (tall, tall, four_tall, four_tall, full, full, full, turned, turned),
        scratch=[pltpu.VMEM(tall.shape, F32)] * 2,
    )(px, ct, mixed, back, dec, wgt)
    received = {key: partner(payload, *key) for key, payload in zip(order, sent)}
    split = rows == 4 and cols == 4 and channels == 128 and expand == 256
    if split:
        grads = (jax.ShapeDtypeStruct((4, 4, 48, 128), F32),)
    else:
        grads = (
            jax.ShapeDtypeStruct((channels, 2 * expand), F32),
            jax.ShapeDtypeStruct((channels, expand), F32),
        )
    outs = vmem_call(
        functools.partial(join_body, (height, breadth), split, order),
        (jax.ShapeDtypeStruct((count, 2 * expand), BF16), *grads, jax.ShapeDtypeStruct((count, expand), BF16)),
    )(rt, *received.values(), s_loc, g_loc, pre, suf, m_in, m_gate, gated, x_t, c_t)
    mix, grads = outs[0], outs[1:-1]
    grad_pixels = vmem_call(pixels_body, like(pixels), kept=False)(ct, mix, w_in)
    if split:
        parts = spread(grads[0], "cols", (1, 2, 3))
        value = (parts[0] + parts[1]) + (parts[2] + parts[3])
        parts = spread(value, "rows", (1, 2, 3))
        grad_in, grad_out = vmem_call(
            final_body, (jax.ShapeDtypeStruct((32, 128), F32), jax.ShapeDtypeStruct((32, 64), F32)), kept=False
        )(*parts)
        return grad_pixels, grad_in, jnp.transpose(grad_out)
    full_in, full_out = grads[0], jnp.transpose(grads[1])
    full_in = lax.psum_scatter(full_in, "cols", scatter_dimension=1, tiled=True)
    full_out = lax.psum_scatter(full_out, "cols", scatter_dimension=1, tiled=True)
    return (
        grad_pixels,
        lax.psum_scatter(full_in, "rows", scatter_dimension=0, tiled=True),
        lax.psum_scatter(full_out, "rows", scatter_dimension=0, tiled=True),
    )


def solution(mesh):
    return jax.shard_map(
        per_device,
        mesh=mesh,
        in_specs=(
            P(("groups", "rows"), "cols", None),
            P(("groups", "rows"), "cols", None),
            P(),
            P(),
            P(),
            P(None, ("groups", "rows"), "cols"),
        ),
        out_specs=(
            P(("groups", "rows"), "cols", None),
            P(("groups", "rows"), "cols"),
            P(("groups", "rows"), "cols"),
        ),
        check_vma=False,
    )
```

```python
import functools

import jax
import jax.numpy as jnp
from jax import lax
from jax.experimental import pallas as pl
from jax.experimental.pallas import tpu as pltpu
from jax.sharding import PartitionSpec as P

F32 = jnp.float32
BF16 = jnp.bfloat16
contract_rows = (((0,), (0,)), ((), ()))
contract_cols = (((1,), (1,)), ((), ()))
VMEM_LIMIT = 6 * 1024 * 1024


def vmem_call(body, out_shape, scratch=(), given=pltpu.VMEM, kept=True):
    spec = pl.BlockSpec(memory_space=pltpu.VMEM)
    if kept:
        out_shape = jax.tree.map(lambda s: pltpu.VMEM(s.shape, s.dtype), out_shape)

    def call(*operands):
        operands = [pltpu.with_memory_space_constraint(a, given) for a in operands]
        return pl.pallas_call(
            body,
            out_shape=out_shape,
            in_specs=[pl.BlockSpec(memory_space=given)] * len(operands),
            out_specs=jax.tree.map(lambda _: spec, out_shape),
            scratch_shapes=scratch,
            compiler_params=pltpu.CompilerParams(vmem_limit_bytes=VMEM_LIMIT),
            cost_estimate=pl.CostEstimate(flops=0, bytes_accessed=0, transcendentals=0),
        )(*operands)

    return call


def get(ref, rows):
    return jnp.concatenate([ref[k, rows, :] for k in range(ref.shape[0])], axis=1)


def put(ref, rows, value):
    for k in range(ref.shape[0]):
        ref[k, rows, :] = value[:, 128 * k : 128 * k + 128]


def sigmoid(value):
    return 0.5 * jnp.tanh(0.5 * value) + 0.5


def decay_pair(rate, step):
    decay = jnp.exp(-(rate * step))
    rest = 1.0 - decay * decay
    return decay, rest * lax.rsqrt(rest)


def pack_column(column):
    pieces = column.shape[0] // 8
    lane = lax.broadcasted_iota(jnp.int32, (8, 128), 1)
    packed = jnp.broadcast_to(column[0:8], (8, 128))
    for k in range(1, pieces):
        packed = jnp.where(lane < k * (128 // pieces), packed, column[8 * k : 8 * k + 8])
    return packed


def pack_states(out, one, two):
    lines = one.shape[0]
    both = jnp.concatenate([one, two], axis=1)
    for k in range(both.shape[1] // 128):
        out[k * lines : (k + 1) * lines, :] = both[:, 128 * k : 128 * k + 128]


def unpack(part, lines, expand):
    tiles = 2 * expand // 128
    states = jnp.concatenate([part[k * lines : (k + 1) * lines, :] for k in range(tiles)], axis=1)
    packed = part[tiles * lines :, :]
    pieces = 2 * lines // 8
    columns = [
        jnp.broadcast_to(packed[:, k * (128 // pieces) : k * (128 // pieces) + 1], (8, expand)) for k in range(pieces)
    ]
    half = pieces // 2
    sums = [jnp.concatenate(columns[d * half : (d + 1) * half], axis=0) for d in (0, 1)]
    return states, jnp.concatenate(sums, axis=1)


def edges_body(order, px_in, ct_in, wi_in, wo_in, rt_in, ss_in, *refs):
    sent = refs[: len(order)]
    px, ct, rt, mixed, back, dec, wgt, wi, wo, ss, src, seed, src_lines, seed_lines, ways, sems = refs[len(order) :]
    pairs = ((ss_in, ss), (rt_in, rt), (px_in, px), (wi_in, wi), (ct_in, ct), (wo_in, wo))
    copies = [pltpu.make_async_copy(a, b, sems.at[k]) for k, (a, b) in enumerate(pairs)]
    for copy in copies:
        copy.start()
    height, breadth, channels = px.shape
    expand = wo.shape[0]
    count = height * breadth
    copies[0].wait()
    copies[1].wait()
    for axis, length, lines in ((0, breadth, height), (1, height, breadth)):
        one, two = 2 * axis, 2 * axis + 1
        steps = {d: ss[d] if axis == 0 else jnp.transpose(ss[d]) for d in (one, two)}
        for i in range(length):
            rows = slice(i * lines, (i + 1) * lines)
            for d, step in steps.items():
                dec[d, rows, :], wgt[d, rows, :] = decay_pair(rt[d : d + 1, :], step[:, i : i + 1])
        sums = jnp.concatenate([jnp.sum(step, axis=1, keepdims=True) for step in steps.values()], axis=0)
        for way in (0, 1):
            ways[axis, way, 2 * lines * expand // 128 :, :] = pack_column(sums)
    for copy in copies[2:]:
        copy.wait()
    both = jnp.dot(px[...].reshape(count, channels), wi[...], preferred_element_type=F32)
    mixed[...] = both
    inner, gate = both[:, :expand], both[:, expand:]
    put(src, slice(None), inner * sigmoid(inner))
    cot = ct[...].reshape(count, channels)
    bg = lax.dot_general(cot, wo[...], contract_cols, preferred_element_type=F32)
    back[...] = bg
    put(seed, slice(None), bg * (gate * sigmoid(gate)))
    for axis, name in ((0, "cols"), (1, "rows")):
        payload = ways.at[axis]
        one, two = 2 * axis, 2 * axis + 1
        length = breadth if axis == 0 else height
        lines = height if axis == 0 else breadth

        if axis == 0:
            for i in range(length):
                for ref, line_ref in ((src, src_lines), (seed, seed_lines)):
                    put(line_ref, pl.ds(i * lines, lines), get(ref, pl.ds(i, lines, stride=length)))
            source, grad = src_lines, seed_lines
        else:
            source, grad = src, seed

        fwd = jnp.zeros((lines, expand), F32)
        adj = jnp.zeros((lines, expand), F32)
        for i in range(length):
            rows = slice(i * lines, (i + 1) * lines)
            fwd = dec[one, rows, :] * fwd + wgt[one, rows, :] * get(source, rows)
            adj = dec[two, rows, :] * (adj + get(grad, rows))
        pack_states(payload.at[0], fwd, adj)
        fwd = jnp.zeros((lines, expand), F32)
        adj = jnp.zeros((lines, expand), F32)
        for i in reversed(range(length)):
            rows = slice(i * lines, (i + 1) * lines)
            fwd = dec[two, rows, :] * fwd + wgt[two, rows, :] * get(source, rows)
            adj = dec[one, rows, :] * (adj + get(grad, rows))
        pack_states(payload.at[1], adj, fwd)
        mine = lax.axis_index(name)
        for (out_axis, k), out in zip(order, sent):
            if out_axis == name:
                out[...] = payload[((mine ^ k) < mine).astype(jnp.int32)]


def local_body(px, ct, mixed, back, dec, wgt, s_loc, g_loc, pre, suf, m_in, m_gate, gated, x_t, c_t, src, seed):
    height, breadth, channels = px.shape
    expand = src.shape[0] * 128
    count = height * breadth
    inner, gate = mixed[:, :expand], mixed[:, expand:]
    s_in, s_gate = sigmoid(inner), sigmoid(gate)
    gate_silu = gate * s_gate
    put(src, slice(None), inner * s_in)
    put(seed, slice(None), back[...] * gate_silu)
    m_in[...] = s_in * (1.0 + inner * (1.0 - s_in))
    gated[...] = gate_silu
    m_gate[...] = back[...] * (s_gate * (1.0 + gate * (1.0 - s_gate)))
    x_t[...] = jnp.transpose(px[...].reshape(count, channels).astype(F32)).astype(BF16)
    c_t[...] = jnp.transpose(ct[...].reshape(count, channels).astype(F32)).astype(BF16)
    for axis in (0, 1):
        one, two = 2 * axis, 2 * axis + 1
        length = breadth if axis == 0 else height
        lines = height if axis == 0 else breadth

        def where(i):
            if axis == 0:
                return pl.ds(i, lines, stride=length)
            return pl.ds(i * lines, lines)

        def go(order, a, b, first):
            state = jnp.zeros((lines, expand), F32)
            carried = jnp.zeros((lines, expand), F32)
            upto = jnp.ones((lines, expand), F32)
            after = jnp.ones((lines, expand), F32)
            for i in order:
                rows = slice(i * lines, (i + 1) * lines)
                da, wa, db, wb = dec[a, rows, :], wgt[a, rows, :], dec[b, rows, :], wgt[b, rows, :]
                state = da * state + wa * get(src, where(i))
                upto = upto * da
                adjoint = get(seed, where(i)) + carried
                carried = db * adjoint
                put(pre.at[a], where(i), upto)
                put(suf.at[b], where(i), wb * after)
                after = after * db
                grad = wb * adjoint
                if not first:
                    state_sum, grad = get(s_loc, where(i)) + state, get(g_loc, where(i)) + grad
                else:
                    state_sum = state
                put(s_loc, where(i), state_sum)
                put(g_loc, where(i), grad)

        go(range(length), one, two, axis == 0)
        go(reversed(range(length)), two, one, False)


def entering(axis, rates, received):
    parts = [received[key] for key in sorted(received) if key[0] == axis]
    count, mine = len(parts) + 1, lax.axis_index(axis)
    expand = rates[0].shape[1]
    lines = (parts[0].shape[0] - 8) * 128 // (2 * expand)
    parts, sums = zip(*(unpack(part, lines, expand) for part in parts))
    both = jnp.concatenate(rates, axis=1)
    below = jnp.zeros((lines, 2 * expand), F32)
    above = jnp.zeros((lines, 2 * expand), F32)
    for k in range(1, count):
        place = mine ^ k
        between = jnp.zeros((lines, 2 * expand), F32)
        for m in range(1, count):
            if m == k:
                continue
            middle = mine ^ m
            inside = ((middle - mine) * (middle - place) < 0).astype(F32)
            between = between + inside * sums[m - 1]
        value = jnp.exp(-both * between) * parts[k - 1]
        lower = (place < mine).astype(F32)
        below = below + lower * value
        above = above + (1.0 - lower) * value
    return below, above


def join_body(shape, split, order, rt, *refs):
    height, breadth = shape
    received = {key: ref[...] for key, ref in zip(order, refs)}
    s_loc, g_loc, pre, suf, m_in, m_gate, gated, x_t, c_t, mix = refs[len(order) : len(order) + 10]
    *grads, out_state = refs[len(order) + 10 :]
    expand = s_loc.shape[0] * 128
    rates = [rt[d : d + 1, :] for d in range(4)]
    below, above = entering("rows", rates[2:], received)
    f2, a3, a2, f3 = below[:, :expand], below[:, expand:], above[:, :expand], above[:, expand:]
    below, above = entering("cols", rates[:2], received)
    for h in range(height):
        rows = slice(h * breadth, (h + 1) * breadth)
        f0, a1 = below[h : h + 1, :expand], below[h : h + 1, expand:]
        a0, f1 = above[h : h + 1, :expand], above[h : h + 1, expand:]
        total, grad = get(s_loc, rows), get(g_loc, rows)
        for d, (state_in, adjoint_in) in enumerate(((f0, a0), (f1, a1), (f2, a2), (f3, a3))):
            total = total + get(pre.at[d], rows) * state_in
            grad = grad + get(suf.at[d], rows) * adjoint_in
        out_state[rows, :] = (total * gated[rows, :]).astype(BF16)
        mix[rows, :expand] = (grad * m_in[rows, :]).astype(BF16)
        mix[rows, expand:] = (total * m_gate[rows, :]).astype(BF16)
    grad_in = jnp.dot(x_t[...], mix[...], preferred_element_type=F32)
    grad_out = jnp.dot(c_t[...], out_state[...], preferred_element_type=F32)
    if not split:
        grads[0][...] = grad_in
        grads[1][...] = grad_out
        return
    packed = grads[0]
    lane = lax.broadcasted_iota(jnp.int32, (16, 128), 1)
    for c in range(4):
        for t in range(2):
            top = grad_out[32 * c : 32 * c + 16, 128 * t : 128 * t + 128]
            bottom = grad_out[32 * c + 16 : 32 * c + 32, 128 * t : 128 * t + 128]
            low = jnp.where(lane < 64, top, pltpu.roll(bottom, 64, 1))
            high = jnp.where(lane < 64, pltpu.roll(top, 64, 1), bottom)
            for k, piece in ((0, low), (1, high)):
                r = 2 * t + k
                packed[c, r, 0:32, :] = grad_in[32 * r : 32 * r + 32, 128 * c : 128 * c + 128]
                packed[c, r, 32:48, :] = piece


def pixels_body(ct, mix, wi, out):
    height, breadth, channels = ct.shape
    grad = lax.dot_general(mix[...], wi[...], contract_cols, preferred_element_type=F32)
    cot = ct[...].reshape(height * breadth, channels).astype(F32)
    out[...] = (cot + grad).astype(BF16).reshape(height, breadth, channels)


def final_body(mine, one, two, three, g_in, g_out):
    total = (mine[...] + one[...]) + (two[...] + three[...])
    g_in[...] = total[0:32, :]
    g_out[0:16, :] = total[32:48, 0:64]
    g_out[16:32, :] = total[32:48, 64:128]


def partner(value, axis, bit):
    return lax.ppermute(value, axis, [(i, i ^ bit) for i in range(lax.axis_size(axis))])


def send_order(cols, rows):
    return [("rows", k) for k in reversed(range(1, rows))] + [("cols", k) for k in reversed(range(1, cols))]


def shifted(value, axis, k):
    count = lax.axis_size(axis)
    return lax.ppermute(value, axis, [(i, (i + k) % count) for i in range(count)])


def spread(value, axis, order):
    count, mine = lax.axis_size(axis), lax.axis_index(axis)
    pick = lambda i: lax.dynamic_index_in_dim(value, i, 0, keepdims=False)
    return [pick(mine)] + [shifted(pick(lax.rem(mine + k, count)), axis, k) for k in order]


def per_device(pixels, cotangent, w_in, w_out, decay_rates, step_sizes):
    height, breadth, channels = pixels.shape
    expand = w_out.shape[0]
    count = height * breadth
    rows, cols = lax.axis_size("rows"), lax.axis_size("cols")
    full = jax.ShapeDtypeStruct((count, expand), F32)
    tall = jax.ShapeDtypeStruct((expand // 128, count, 128), F32)
    four_tall = jax.ShapeDtypeStruct((4, expand // 128, count, 128), F32)
    four = jax.ShapeDtypeStruct((4, count, expand), F32)
    wide = jax.ShapeDtypeStruct((count, 2 * expand), F32)
    like = lambda a: jax.ShapeDtypeStruct(a.shape, a.dtype)
    pay_cols, pay_rows = (
        jax.ShapeDtypeStruct((2 * lines * expand // 128 + 8, 128), F32) for lines in (height, breadth)
    )
    order = send_order(cols, rows)
    pays = tuple(pay_cols if axis == "cols" else pay_rows for axis, _ in order)
    outs = vmem_call(
        functools.partial(edges_body, order),
        (*pays, like(pixels), like(cotangent), like(decay_rates), wide, full, four, four),
        scratch=[
            pltpu.VMEM(w_in.shape, BF16),
            pltpu.VMEM(w_out.shape, BF16),
            pltpu.VMEM(step_sizes.shape, F32),
            *(pltpu.VMEM(tall.shape, F32) for _ in range(4)),
            pltpu.VMEM((2, 2, *pay_cols.shape), F32),
            pltpu.SemaphoreType.DMA((6,)),
        ],
        given=pltpu.HBM,
    )(pixels, cotangent, w_in, w_out, decay_rates, step_sizes)
    sent = outs[: len(pays)]
    px, ct, rt, mixed, back, dec, wgt = outs[len(pays) :]
    turned = jax.ShapeDtypeStruct((channels, count), BF16)
    s_loc, g_loc, pre, suf, m_in, m_gate, gated, x_t, c_t = vmem_call(
        local_body,
        (tall, tall, four_tall, four_tall, full, full, full, turned, turned),
        scratch=[pltpu.VMEM(tall.shape, F32)] * 2,
    )(px, ct, mixed, back, dec, wgt)
    received = {key: partner(payload, *key) for key, payload in zip(order, sent)}
    split = rows == 4 and cols == 4 and channels == 128 and expand == 256
    if split:
        grads = (jax.ShapeDtypeStruct((4, 4, 48, 128), F32),)
    else:
        grads = (
            jax.ShapeDtypeStruct((channels, 2 * expand), F32),
            jax.ShapeDtypeStruct((channels, expand), F32),
        )
    outs = vmem_call(
        functools.partial(join_body, (height, breadth), split, order),
        (jax.ShapeDtypeStruct((count, 2 * expand), BF16), *grads),
        scratch=[pltpu.VMEM((count, expand), BF16)],
    )(rt, *received.values(), s_loc, g_loc, pre, suf, m_in, m_gate, gated, x_t, c_t)
    mix, grads = outs[0], outs[1:]
    grad_pixels = vmem_call(pixels_body, like(pixels), kept=False)(ct, mix, w_in)
    if split:
        parts = spread(grads[0], "cols", (1, 2, 3))
        value = (parts[0] + parts[1]) + (parts[2] + parts[3])
        parts = spread(value, "rows", (1, 2, 3))
        grad_in, grad_out = vmem_call(
            final_body, (jax.ShapeDtypeStruct((32, 128), F32), jax.ShapeDtypeStruct((32, 64), F32)), kept=False
        )(*parts)
        return grad_pixels, grad_in, jnp.transpose(grad_out)
    full_in, full_out = grads[0], jnp.transpose(grads[1])
    full_in = lax.psum_scatter(full_in, "cols", scatter_dimension=1, tiled=True)
    full_out = lax.psum_scatter(full_out, "cols", scatter_dimension=1, tiled=True)
    return (
        grad_pixels,
        lax.psum_scatter(full_in, "rows", scatter_dimension=0, tiled=True),
        lax.psum_scatter(full_out, "rows", scatter_dimension=0, tiled=True),
    )


def solution(mesh):
    return jax.shard_map(
        per_device,
        mesh=mesh,
        in_specs=(
            P(("groups", "rows"), "cols", None),
            P(("groups", "rows"), "cols", None),
            P(),
            P(),
            P(),
            P(None, ("groups", "rows"), "cols"),
        ),
        out_specs=(
            P(("groups", "rows"), "cols", None),
            P(("groups", "rows"), "cols"),
            P(("groups", "rows"), "cols"),
        ),
        check_vma=False,
    )
```

```python
import functools

import jax
import jax.numpy as jnp
from jax import lax
from jax.experimental import pallas as pl
from jax.experimental.pallas import tpu as pltpu
from jax.sharding import PartitionSpec as P

F32 = jnp.float32
BF16 = jnp.bfloat16
contract_rows = (((0,), (0,)), ((), ()))
contract_cols = (((1,), (1,)), ((), ()))
VMEM_LIMIT = 6 * 1024 * 1024


def vmem_call(body, out_shape, scratch=(), given=pltpu.VMEM, kept=True):
    spec = pl.BlockSpec(memory_space=pltpu.VMEM)
    if kept:
        out_shape = jax.tree.map(lambda s: pltpu.VMEM(s.shape, s.dtype), out_shape)

    def call(*operands):
        operands = [pltpu.with_memory_space_constraint(a, given) for a in operands]
        return pl.pallas_call(
            body,
            out_shape=out_shape,
            in_specs=[pl.BlockSpec(memory_space=given)] * len(operands),
            out_specs=jax.tree.map(lambda _: spec, out_shape),
            scratch_shapes=scratch,
            compiler_params=pltpu.CompilerParams(vmem_limit_bytes=VMEM_LIMIT),
            cost_estimate=pl.CostEstimate(flops=0, bytes_accessed=0, transcendentals=0),
        )(*operands)

    return call


def get(ref, rows):
    return jnp.concatenate([ref[k, rows, :] for k in range(ref.shape[0])], axis=1)


def put(ref, rows, value):
    for k in range(ref.shape[0]):
        ref[k, rows, :] = value[:, 128 * k : 128 * k + 128]


def sigmoid(value):
    return 0.5 * jnp.tanh(0.5 * value) + 0.5


def decay_pair(rate, step):
    decay = jnp.exp(-(rate * step))
    rest = 1.0 - decay * decay
    return decay, rest * lax.rsqrt(rest)


def pack_column(column):
    pieces = column.shape[0] // 8
    lane = lax.broadcasted_iota(jnp.int32, (8, 128), 1)
    packed = jnp.broadcast_to(column[0:8], (8, 128))
    for k in range(1, pieces):
        packed = jnp.where(lane < k * (128 // pieces), packed, column[8 * k : 8 * k + 8])
    return packed


def pack_states(out, one, two):
    lines = one.shape[0]
    both = jnp.concatenate([one, two], axis=1)
    for k in range(both.shape[1] // 128):
        out[k * lines : (k + 1) * lines, :] = both[:, 128 * k : 128 * k + 128]


def unpack(part, lines, expand):
    tiles = 2 * expand // 128
    states = jnp.concatenate([part[k * lines : (k + 1) * lines, :] for k in range(tiles)], axis=1)
    packed = part[tiles * lines :, :]
    pieces = 2 * lines // 8
    columns = [
        jnp.broadcast_to(packed[:, k * (128 // pieces) : k * (128 // pieces) + 1], (8, expand)) for k in range(pieces)
    ]
    half = pieces // 2
    sums = [jnp.concatenate(columns[d * half : (d + 1) * half], axis=0) for d in (0, 1)]
    return states, jnp.concatenate(sums, axis=1)


def edges_body(order, px_in, ct_in, wi_in, wo_in, rt_in, ss_in, *refs):
    sent = refs[: len(order)]
    px, ct, rt, mixed, back, dec, wgt, wi, wo, ss, src, seed, src_lines, seed_lines, ways, sems = refs[len(order) :]
    pairs = ((ss_in, ss), (rt_in, rt), (px_in, px), (wi_in, wi), (ct_in, ct), (wo_in, wo))
    copies = [pltpu.make_async_copy(a, b, sems.at[k]) for k, (a, b) in enumerate(pairs)]
    for copy in copies:
        copy.start()
    height, breadth, channels = px.shape
    expand = wo.shape[0]
    count = height * breadth
    copies[0].wait()
    copies[1].wait()
    for axis, length, lines in ((0, breadth, height), (1, height, breadth)):
        one, two = 2 * axis, 2 * axis + 1
        steps = {d: ss[d] if axis == 0 else jnp.transpose(ss[d]) for d in (one, two)}
        for i in range(length):
            rows = slice(i * lines, (i + 1) * lines)
            for d, step in steps.items():
                dec[d, rows, :], wgt[d, rows, :] = decay_pair(rt[d : d + 1, :], step[:, i : i + 1])
        sums = jnp.concatenate([jnp.sum(step, axis=1, keepdims=True) for step in steps.values()], axis=0)
        for way in (0, 1):
            ways[axis, way, 2 * lines * expand // 128 :, :] = pack_column(sums)
    for copy in copies[2:]:
        copy.wait()
    both = jnp.dot(px[...].reshape(count, channels), wi[...], preferred_element_type=F32)
    mixed[...] = both
    inner, gate = both[:, :expand], both[:, expand:]
    put(src, slice(None), inner * sigmoid(inner))
    cot = ct[...].reshape(count, channels)
    bg = lax.dot_general(cot, wo[...], contract_cols, preferred_element_type=F32)
    back[...] = bg
    put(seed, slice(None), bg * (gate * sigmoid(gate)))
    for axis, name in ((0, "cols"), (1, "rows")):
        payload = ways.at[axis]
        one, two = 2 * axis, 2 * axis + 1
        length = breadth if axis == 0 else height
        lines = height if axis == 0 else breadth

        if axis == 0:
            for i in range(length):
                for ref, line_ref in ((src, src_lines), (seed, seed_lines)):
                    put(line_ref, pl.ds(i * lines, lines), get(ref, pl.ds(i, lines, stride=length)))
            source, grad = src_lines, seed_lines
        else:
            source, grad = src, seed

        fwd = jnp.zeros((lines, expand), F32)
        adj = jnp.zeros((lines, expand), F32)
        for i in range(length):
            rows = slice(i * lines, (i + 1) * lines)
            fwd = dec[one, rows, :] * fwd + wgt[one, rows, :] * get(source, rows)
            adj = dec[two, rows, :] * (adj + get(grad, rows))
        pack_states(payload.at[0], fwd, adj)
        fwd = jnp.zeros((lines, expand), F32)
        adj = jnp.zeros((lines, expand), F32)
        for i in reversed(range(length)):
            rows = slice(i * lines, (i + 1) * lines)
            fwd = dec[two, rows, :] * fwd + wgt[two, rows, :] * get(source, rows)
            adj = dec[one, rows, :] * (adj + get(grad, rows))
        pack_states(payload.at[1], adj, fwd)
        mine, count_of = lax.axis_index(name), 1 + sum(key[0] == name for key in order)
        for (out_axis, kind, k), out in zip(order, sent):
            if out_axis == name:
                out[...] = payload[(target(mine, kind, k, count_of) < mine).astype(jnp.int32)]


def local_body(px, ct, mixed, back, dec, wgt, s_loc, g_loc, pre, suf, m_in, m_gate, gated, x_t, c_t, src, seed):
    height, breadth, channels = px.shape
    expand = src.shape[0] * 128
    count = height * breadth
    inner, gate = mixed[:, :expand], mixed[:, expand:]
    s_in, s_gate = sigmoid(inner), sigmoid(gate)
    gate_silu = gate * s_gate
    put(src, slice(None), inner * s_in)
    put(seed, slice(None), back[...] * gate_silu)
    m_in[...] = s_in * (1.0 + inner * (1.0 - s_in))
    gated[...] = gate_silu
    m_gate[...] = back[...] * (s_gate * (1.0 + gate * (1.0 - s_gate)))
    x_t[...] = jnp.transpose(px[...].reshape(count, channels).astype(F32)).astype(BF16)
    c_t[...] = jnp.transpose(ct[...].reshape(count, channels).astype(F32)).astype(BF16)
    for axis in (0, 1):
        one, two = 2 * axis, 2 * axis + 1
        length = breadth if axis == 0 else height
        lines = height if axis == 0 else breadth

        def where(i):
            if axis == 0:
                return pl.ds(i, lines, stride=length)
            return pl.ds(i * lines, lines)

        def go(order, a, b, first):
            state = jnp.zeros((lines, expand), F32)
            carried = jnp.zeros((lines, expand), F32)
            upto = jnp.ones((lines, expand), F32)
            after = jnp.ones((lines, expand), F32)
            for i in order:
                rows = slice(i * lines, (i + 1) * lines)
                da, wa, db, wb = dec[a, rows, :], wgt[a, rows, :], dec[b, rows, :], wgt[b, rows, :]
                state = da * state + wa * get(src, where(i))
                upto = upto * da
                adjoint = get(seed, where(i)) + carried
                carried = db * adjoint
                put(pre.at[a], where(i), upto)
                put(suf.at[b], where(i), wb * after)
                after = after * db
                grad = wb * adjoint
                if not first:
                    state_sum, grad = get(s_loc, where(i)) + state, get(g_loc, where(i)) + grad
                else:
                    state_sum = state
                put(s_loc, where(i), state_sum)
                put(g_loc, where(i), grad)

        go(range(length), one, two, axis == 0)
        go(reversed(range(length)), two, one, False)


def target(mine, kind, k, count):
    if kind == "xor":
        return mine ^ k
    place = mine + k
    return jnp.where(place < count, place, place - count)


def entering(axis, rates, received):
    keys = [key for key in received if key[0] == axis]
    parts = [received[key] for key in keys]
    count, mine = len(parts) + 1, lax.axis_index(axis)
    expand = rates[0].shape[1]
    lines = (parts[0].shape[0] - 8) * 128 // (2 * expand)
    parts, sums = zip(*(unpack(part, lines, expand) for part in parts))
    places = [target(mine, kind, k if kind == "xor" else count - k, count) for _, kind, k in keys]
    both = jnp.concatenate(rates, axis=1)
    below = jnp.zeros((lines, 2 * expand), F32)
    above = jnp.zeros((lines, 2 * expand), F32)
    for k, place in enumerate(places):
        between = jnp.zeros((lines, 2 * expand), F32)
        for m, middle in enumerate(places):
            if m != k:
                inside = ((middle - mine) * (middle - place) < 0).astype(F32)
                between = between + inside * sums[m]
        value = jnp.exp(-both * between) * parts[k]
        lower = (place < mine).astype(F32)
        below = below + lower * value
        above = above + (1.0 - lower) * value
    return below, above


def join_body(shape, split, order, rt, *refs):
    height, breadth = shape
    received = {key: ref[...] for key, ref in zip(order, refs)}
    s_loc, g_loc, pre, suf, m_in, m_gate, gated, x_t, c_t, mix = refs[len(order) : len(order) + 10]
    *grads, out_state = refs[len(order) + 10 :]
    expand = s_loc.shape[0] * 128
    rates = [rt[d : d + 1, :] for d in range(4)]
    below, above = entering("rows", rates[2:], received)
    f2, a3, a2, f3 = below[:, :expand], below[:, expand:], above[:, :expand], above[:, expand:]
    below, above = entering("cols", rates[:2], received)
    for h in range(height):
        rows = slice(h * breadth, (h + 1) * breadth)
        f0, a1 = below[h : h + 1, :expand], below[h : h + 1, expand:]
        a0, f1 = above[h : h + 1, :expand], above[h : h + 1, expand:]
        total, grad = get(s_loc, rows), get(g_loc, rows)
        for d, (state_in, adjoint_in) in enumerate(((f0, a0), (f1, a1), (f2, a2), (f3, a3))):
            total = total + get(pre.at[d], rows) * state_in
            grad = grad + get(suf.at[d], rows) * adjoint_in
        out_state[rows, :] = (total * gated[rows, :]).astype(BF16)
        mix[rows, :expand] = (grad * m_in[rows, :]).astype(BF16)
        mix[rows, expand:] = (total * m_gate[rows, :]).astype(BF16)
    grad_in = jnp.dot(x_t[...], mix[...], preferred_element_type=F32)
    grad_out = jnp.dot(c_t[...], out_state[...], preferred_element_type=F32)
    if not split:
        grads[0][...] = grad_in
        grads[1][...] = grad_out
        return
    packed = grads[0]
    lane = lax.broadcasted_iota(jnp.int32, (16, 128), 1)
    for c in range(4):
        for t in range(2):
            top = grad_out[32 * c : 32 * c + 16, 128 * t : 128 * t + 128]
            bottom = grad_out[32 * c + 16 : 32 * c + 32, 128 * t : 128 * t + 128]
            low = jnp.where(lane < 64, top, pltpu.roll(bottom, 64, 1))
            high = jnp.where(lane < 64, pltpu.roll(top, 64, 1), bottom)
            for k, piece in ((0, low), (1, high)):
                r = 2 * t + k
                packed[c, r, 0:32, :] = grad_in[32 * r : 32 * r + 32, 128 * c : 128 * c + 128]
                packed[c, r, 32:48, :] = piece


def pixels_body(ct, mix, wi, out):
    height, breadth, channels = ct.shape
    grad = lax.dot_general(mix[...], wi[...], contract_cols, preferred_element_type=F32)
    cot = ct[...].reshape(height * breadth, channels).astype(F32)
    out[...] = (cot + grad).astype(BF16).reshape(height, breadth, channels)


def final_body(mine, one, two, three, g_in, g_out):
    total = (mine[...] + one[...]) + (two[...] + three[...])
    g_in[...] = total[0:32, :]
    g_out[0:16, :] = total[32:48, 0:64]
    g_out[16:32, :] = total[32:48, 64:128]


def send_order(cols, rows):
    near = sorted(range(1, rows), key=lambda k: min(k, rows - k))
    return [("rows", "shift", k) for k in near] + [("cols", "xor", k) for k in reversed(range(1, cols))]


def transfer(value, axis, kind, k):
    count = lax.axis_size(axis)
    return lax.ppermute(value, axis, [(i, i ^ k if kind == "xor" else (i + k) % count) for i in range(count)])


def spread(value, axis, order):
    count, mine = lax.axis_size(axis), lax.axis_index(axis)
    pick = lambda i: lax.dynamic_index_in_dim(value, i, 0, keepdims=False)
    return [pick(mine)] + [transfer(pick(target(mine, kind, k, count)), axis, kind, k) for kind, k in order]


def per_device(pixels, cotangent, w_in, w_out, decay_rates, step_sizes):
    height, breadth, channels = pixels.shape
    expand = w_out.shape[0]
    count = height * breadth
    rows, cols = lax.axis_size("rows"), lax.axis_size("cols")
    full = jax.ShapeDtypeStruct((count, expand), F32)
    tall = jax.ShapeDtypeStruct((expand // 128, count, 128), F32)
    four_tall = jax.ShapeDtypeStruct((4, expand // 128, count, 128), F32)
    four = jax.ShapeDtypeStruct((4, count, expand), F32)
    wide = jax.ShapeDtypeStruct((count, 2 * expand), F32)
    like = lambda a: jax.ShapeDtypeStruct(a.shape, a.dtype)
    pay_cols, pay_rows = (
        jax.ShapeDtypeStruct((2 * lines * expand // 128 + 8, 128), F32) for lines in (height, breadth)
    )
    order = send_order(cols, rows)
    pays = tuple(pay_cols if axis == "cols" else pay_rows for axis, _, _ in order)
    outs = vmem_call(
        functools.partial(edges_body, order),
        (*pays, like(pixels), like(cotangent), like(decay_rates), wide, full, four, four),
        scratch=[
            pltpu.VMEM(w_in.shape, BF16),
            pltpu.VMEM(w_out.shape, BF16),
            pltpu.VMEM(step_sizes.shape, F32),
            *(pltpu.VMEM(tall.shape, F32) for _ in range(4)),
            pltpu.VMEM((2, 2, *pay_cols.shape), F32),
            pltpu.SemaphoreType.DMA((6,)),
        ],
        given=pltpu.HBM,
    )(pixels, cotangent, w_in, w_out, decay_rates, step_sizes)
    sent = outs[: len(pays)]
    px, ct, rt, mixed, back, dec, wgt = outs[len(pays) :]
    turned = jax.ShapeDtypeStruct((channels, count), BF16)
    s_loc, g_loc, pre, suf, m_in, m_gate, gated, x_t, c_t = vmem_call(
        local_body,
        (tall, tall, four_tall, four_tall, full, full, full, turned, turned),
        scratch=[pltpu.VMEM(tall.shape, F32)] * 2,
    )(px, ct, mixed, back, dec, wgt)
    received = {key: transfer(payload, *key) for key, payload in zip(order, sent)}
    split = rows == 4 and cols == 4 and channels == 128 and expand == 256
    if split:
        grads = (jax.ShapeDtypeStruct((4, 4, 48, 128), F32),)
    else:
        grads = (
            jax.ShapeDtypeStruct((channels, 2 * expand), F32),
            jax.ShapeDtypeStruct((channels, expand), F32),
        )
    outs = vmem_call(
        functools.partial(join_body, (height, breadth), split, order),
        (jax.ShapeDtypeStruct((count, 2 * expand), BF16), *grads),
        scratch=[pltpu.VMEM((count, expand), BF16)],
    )(rt, *received.values(), s_loc, g_loc, pre, suf, m_in, m_gate, gated, x_t, c_t)
    mix, grads = outs[0], outs[1:]
    grad_pixels = vmem_call(pixels_body, like(pixels), kept=False)(ct, mix, w_in)
    if split:
        parts = spread(grads[0], "cols", [("shift", k) for k in (1, 2, 3)])
        value = (parts[0] + parts[1]) + (parts[2] + parts[3])
        parts = spread(value, "rows", [("shift", k) for k in (1, 2, 3)])
        grad_in, grad_out = vmem_call(
            final_body, (jax.ShapeDtypeStruct((32, 128), F32), jax.ShapeDtypeStruct((32, 64), F32)), kept=False
        )(*parts)
        return grad_pixels, grad_in, jnp.transpose(grad_out)
    full_in, full_out = grads[0], jnp.transpose(grads[1])
    full_in = lax.psum_scatter(full_in, "cols", scatter_dimension=1, tiled=True)
    full_out = lax.psum_scatter(full_out, "cols", scatter_dimension=1, tiled=True)
    return (
        grad_pixels,
        lax.psum_scatter(full_in, "rows", scatter_dimension=0, tiled=True),
        lax.psum_scatter(full_out, "rows", scatter_dimension=0, tiled=True),
    )


def solution(mesh):
    return jax.shard_map(
        per_device,
        mesh=mesh,
        in_specs=(
            P(("groups", "rows"), "cols", None),
            P(("groups", "rows"), "cols", None),
            P(),
            P(),
            P(),
            P(None, ("groups", "rows"), "cols"),
        ),
        out_specs=(
            P(("groups", "rows"), "cols", None),
            P(("groups", "rows"), "cols"),
            P(("groups", "rows"), "cols"),
        ),
        check_vma=False,
    )
```

```python
import functools

import jax
import jax.numpy as jnp
from jax import lax
from jax.experimental import pallas as pl
from jax.experimental.pallas import tpu as pltpu
from jax.sharding import PartitionSpec as P

F32 = jnp.float32
BF16 = jnp.bfloat16
contract_rows = (((0,), (0,)), ((), ()))
contract_cols = (((1,), (1,)), ((), ()))
VMEM_LIMIT = 6 * 1024 * 1024


def vmem_call(body, out_shape, scratch=(), given=pltpu.VMEM, kept=True):
    spec = pl.BlockSpec(memory_space=pltpu.VMEM)
    if kept:
        out_shape = jax.tree.map(lambda s: pltpu.VMEM(s.shape, s.dtype), out_shape)

    def call(*operands):
        operands = [pltpu.with_memory_space_constraint(a, given) for a in operands]
        return pl.pallas_call(
            body,
            out_shape=out_shape,
            in_specs=[pl.BlockSpec(memory_space=given)] * len(operands),
            out_specs=jax.tree.map(lambda _: spec, out_shape),
            scratch_shapes=scratch,
            compiler_params=pltpu.CompilerParams(vmem_limit_bytes=VMEM_LIMIT),
            cost_estimate=pl.CostEstimate(flops=0, bytes_accessed=0, transcendentals=0),
        )(*operands)

    return call


def get(ref, rows):
    return jnp.concatenate([ref[k, rows, :] for k in range(ref.shape[0])], axis=1)


def put(ref, rows, value):
    for k in range(ref.shape[0]):
        ref[k, rows, :] = value[:, 128 * k : 128 * k + 128]


def sigmoid(value):
    return 0.5 * jnp.tanh(0.5 * value) + 0.5


def decay_pair(rate, step):
    decay = jnp.exp(-(rate * step))
    rest = 1.0 - decay * decay
    return decay, rest * lax.rsqrt(rest)


def pack_column(column):
    pieces = column.shape[0] // 8
    lane = lax.broadcasted_iota(jnp.int32, (8, 128), 1)
    packed = jnp.broadcast_to(column[0:8], (8, 128))
    for k in range(1, pieces):
        packed = jnp.where(lane < k * (128 // pieces), packed, column[8 * k : 8 * k + 8])
    return packed


def pack_states(out, one, two):
    lines = one.shape[0]
    both = jnp.concatenate([one, two], axis=1)
    for k in range(both.shape[1] // 128):
        out[k * lines : (k + 1) * lines, :] = both[:, 128 * k : 128 * k + 128]


def unpack(part, lines, expand):
    tiles = 2 * expand // 128
    states = jnp.concatenate([part[k * lines : (k + 1) * lines, :] for k in range(tiles)], axis=1)
    packed = part[tiles * lines :, :]
    pieces = 2 * lines // 8
    columns = [
        jnp.broadcast_to(packed[:, k * (128 // pieces) : k * (128 // pieces) + 1], (8, expand)) for k in range(pieces)
    ]
    half = pieces // 2
    sums = [jnp.concatenate(columns[d * half : (d + 1) * half], axis=0) for d in (0, 1)]
    return states, jnp.concatenate(sums, axis=1)


def edges_body(order, px_in, ct_in, wi_in, wo_in, rt_in, ss_in, *refs):
    sent = refs[: len(order)]
    px, ct, rt, mixed, back, dec, wgt, wi, wo, ss, src, seed, src_lines, seed_lines, ways, sems = refs[len(order) :]
    pairs = ((wi_in, wi), (px_in, px), (ct_in, ct), (wo_in, wo), (ss_in, ss), (rt_in, rt))
    copies = [pltpu.make_async_copy(a, b, sems.at[k]) for k, (a, b) in enumerate(pairs)]
    for copy in copies:
        copy.start()
    height, breadth, channels = px.shape
    expand = wo.shape[0]
    count = height * breadth
    for copy in copies:
        copy.wait()
    for axis, length, lines in ((0, breadth, height), (1, height, breadth)):
        one, two = 2 * axis, 2 * axis + 1
        steps = {d: ss[d] if axis == 0 else jnp.transpose(ss[d]) for d in (one, two)}
        for i in range(length):
            rows = slice(i * lines, (i + 1) * lines)
            for d, step in steps.items():
                dec[d, rows, :], wgt[d, rows, :] = decay_pair(rt[d : d + 1, :], step[:, i : i + 1])
        sums = jnp.concatenate([jnp.sum(step, axis=1, keepdims=True) for step in steps.values()], axis=0)
        for way in (0, 1):
            ways[axis, way, 2 * lines * expand // 128 :, :] = pack_column(sums)
    both = jnp.dot(px[...].reshape(count, channels), wi[...], preferred_element_type=F32)
    mixed[...] = both
    inner, gate = both[:, :expand], both[:, expand:]
    put(src, slice(None), inner * sigmoid(inner))
    cot = ct[...].reshape(count, channels)
    bg = lax.dot_general(cot, wo[...], contract_cols, preferred_element_type=F32)
    back[...] = bg
    put(seed, slice(None), bg * (gate * sigmoid(gate)))
    for axis, name in ((0, "cols"), (1, "rows")):
        payload = ways.at[axis]
        one, two = 2 * axis, 2 * axis + 1
        length = breadth if axis == 0 else height
        lines = height if axis == 0 else breadth

        if axis == 0:
            for i in range(length):
                for ref, line_ref in ((src, src_lines), (seed, seed_lines)):
                    put(line_ref, pl.ds(i * lines, lines), get(ref, pl.ds(i, lines, stride=length)))
            source, grad = src_lines, seed_lines
        else:
            source, grad = src, seed

        fwd = jnp.zeros((lines, expand), F32)
        adj = jnp.zeros((lines, expand), F32)
        for i in range(length):
            rows = slice(i * lines, (i + 1) * lines)
            fwd = dec[one, rows, :] * fwd + wgt[one, rows, :] * get(source, rows)
            adj = dec[two, rows, :] * (adj + get(grad, rows))
        pack_states(payload.at[0], fwd, adj)
        fwd = jnp.zeros((lines, expand), F32)
        adj = jnp.zeros((lines, expand), F32)
        for i in reversed(range(length)):
            rows = slice(i * lines, (i + 1) * lines)
            fwd = dec[two, rows, :] * fwd + wgt[two, rows, :] * get(source, rows)
            adj = dec[one, rows, :] * (adj + get(grad, rows))
        pack_states(payload.at[1], adj, fwd)
        mine, count_of = lax.axis_index(name), 1 + sum(key[0] == name for key in order)
        for (out_axis, kind, k), out in zip(order, sent):
            if out_axis == name:
                out[...] = payload[(target(mine, kind, k, count_of) < mine).astype(jnp.int32)]


def local_body(px, ct, mixed, back, dec, wgt, s_loc, g_loc, pre, suf, m_in, m_gate, gated, x_t, c_t, src, seed):
    height, breadth, channels = px.shape
    expand = src.shape[0] * 128
    count = height * breadth
    inner, gate = mixed[:, :expand], mixed[:, expand:]
    s_in, s_gate = sigmoid(inner), sigmoid(gate)
    gate_silu = gate * s_gate
    put(src, slice(None), inner * s_in)
    put(seed, slice(None), back[...] * gate_silu)
    m_in[...] = s_in * (1.0 + inner * (1.0 - s_in))
    gated[...] = gate_silu
    m_gate[...] = back[...] * (s_gate * (1.0 + gate * (1.0 - s_gate)))
    x_t[...] = jnp.transpose(px[...].reshape(count, channels).astype(F32)).astype(BF16)
    c_t[...] = jnp.transpose(ct[...].reshape(count, channels).astype(F32)).astype(BF16)
    for axis in (0, 1):
        one, two = 2 * axis, 2 * axis + 1
        length = breadth if axis == 0 else height
        lines = height if axis == 0 else breadth

        def where(i):
            if axis == 0:
                return pl.ds(i, lines, stride=length)
            return pl.ds(i * lines, lines)

        def go(order, a, b, first):
            state = jnp.zeros((lines, expand), F32)
            carried = jnp.zeros((lines, expand), F32)
            upto = jnp.ones((lines, expand), F32)
            after = jnp.ones((lines, expand), F32)
            for i in order:
                rows = slice(i * lines, (i + 1) * lines)
                da, wa, db, wb = dec[a, rows, :], wgt[a, rows, :], dec[b, rows, :], wgt[b, rows, :]
                state = da * state + wa * get(src, where(i))
                upto = upto * da
                adjoint = get(seed, where(i)) + carried
                carried = db * adjoint
                put(pre.at[a], where(i), upto)
                put(suf.at[b], where(i), wb * after)
                after = after * db
                grad = wb * adjoint
                if not first:
                    state_sum, grad = get(s_loc, where(i)) + state, get(g_loc, where(i)) + grad
                else:
                    state_sum = state
                put(s_loc, where(i), state_sum)
                put(g_loc, where(i), grad)

        go(range(length), one, two, axis == 0)
        go(reversed(range(length)), two, one, False)


def target(mine, kind, k, count):
    if kind == "xor":
        return mine ^ k
    place = mine + k
    return jnp.where(place < count, place, place - count)


def entering(axis, rates, received):
    keys = [key for key in received if key[0] == axis]
    parts = [received[key] for key in keys]
    count, mine = len(parts) + 1, lax.axis_index(axis)
    expand = rates[0].shape[1]
    lines = (parts[0].shape[0] - 8) * 128 // (2 * expand)
    parts, sums = zip(*(unpack(part, lines, expand) for part in parts))
    places = [target(mine, kind, k if kind == "xor" else count - k, count) for _, kind, k in keys]
    both = jnp.concatenate(rates, axis=1)
    below = jnp.zeros((lines, 2 * expand), F32)
    above = jnp.zeros((lines, 2 * expand), F32)
    for k, place in enumerate(places):
        between = jnp.zeros((lines, 2 * expand), F32)
        for m, middle in enumerate(places):
            if m != k:
                inside = ((middle - mine) * (middle - place) < 0).astype(F32)
                between = between + inside * sums[m]
        value = jnp.exp(-both * between) * parts[k]
        lower = (place < mine).astype(F32)
        below = below + lower * value
        above = above + (1.0 - lower) * value
    return below, above


def join_body(shape, split, order, rt, *refs):
    height, breadth = shape
    received = {key: ref[...] for key, ref in zip(order, refs)}
    s_loc, g_loc, pre, suf, m_in, m_gate, gated, x_t, c_t, mix = refs[len(order) : len(order) + 10]
    *grads, out_state = refs[len(order) + 10 :]
    expand = s_loc.shape[0] * 128
    rates = [rt[d : d + 1, :] for d in range(4)]
    below, above = entering("rows", rates[2:], received)
    f2, a3, a2, f3 = below[:, :expand], below[:, expand:], above[:, :expand], above[:, expand:]
    below, above = entering("cols", rates[:2], received)
    for h in range(height):
        rows = slice(h * breadth, (h + 1) * breadth)
        f0, a1 = below[h : h + 1, :expand], below[h : h + 1, expand:]
        a0, f1 = above[h : h + 1, :expand], above[h : h + 1, expand:]
        total, grad = get(s_loc, rows), get(g_loc, rows)
        for d, (state_in, adjoint_in) in enumerate(((f0, a0), (f1, a1), (f2, a2), (f3, a3))):
            total = total + get(pre.at[d], rows) * state_in
            grad = grad + get(suf.at[d], rows) * adjoint_in
        out_state[rows, :] = (total * gated[rows, :]).astype(BF16)
        mix[rows, :expand] = (grad * m_in[rows, :]).astype(BF16)
        mix[rows, expand:] = (total * m_gate[rows, :]).astype(BF16)
    grad_in = jnp.dot(x_t[...], mix[...], preferred_element_type=F32)
    grad_out = jnp.dot(c_t[...], out_state[...], preferred_element_type=F32)
    if not split:
        grads[0][...] = grad_in
        grads[1][...] = grad_out
        return
    packed = grads[0]
    lane = lax.broadcasted_iota(jnp.int32, (16, 128), 1)
    for c in range(4):
        for t in range(2):
            top = grad_out[32 * c : 32 * c + 16, 128 * t : 128 * t + 128]
            bottom = grad_out[32 * c + 16 : 32 * c + 32, 128 * t : 128 * t + 128]
            low = jnp.where(lane < 64, top, pltpu.roll(bottom, 64, 1))
            high = jnp.where(lane < 64, pltpu.roll(top, 64, 1), bottom)
            for k, piece in ((0, low), (1, high)):
                r = 2 * t + k
                packed[c, r, 0:32, :] = grad_in[32 * r : 32 * r + 32, 128 * c : 128 * c + 128]
                packed[c, r, 32:48, :] = piece


def pixels_body(ct, mix, wi, out):
    height, breadth, channels = ct.shape
    grad = lax.dot_general(mix[...], wi[...], contract_cols, preferred_element_type=F32)
    cot = ct[...].reshape(height * breadth, channels).astype(F32)
    out[...] = (cot + grad).astype(BF16).reshape(height, breadth, channels)


def final_body(mine, one, two, three, g_in, g_out):
    total = (mine[...] + one[...]) + (two[...] + three[...])
    g_in[...] = total[0:32, :]
    g_out[0:16, :] = total[32:48, 0:64]
    g_out[16:32, :] = total[32:48, 64:128]


def send_order(cols, rows):
    near = sorted(range(1, rows), key=lambda k: min(k, rows - k))
    return [("rows", "shift", k) for k in near] + [("cols", "xor", k) for k in reversed(range(1, cols))]


def transfer(value, axis, kind, k):
    count = lax.axis_size(axis)
    return lax.ppermute(value, axis, [(i, i ^ k if kind == "xor" else (i + k) % count) for i in range(count)])


def spread(value, axis, order):
    count, mine = lax.axis_size(axis), lax.axis_index(axis)
    pick = lambda i: lax.dynamic_index_in_dim(value, i, 0, keepdims=False)
    return [pick(mine)] + [transfer(pick(target(mine, kind, k, count)), axis, kind, k) for kind, k in order]


def per_device(pixels, cotangent, w_in, w_out, decay_rates, step_sizes):
    height, breadth, channels = pixels.shape
    expand = w_out.shape[0]
    count = height * breadth
    rows, cols = lax.axis_size("rows"), lax.axis_size("cols")
    full = jax.ShapeDtypeStruct((count, expand), F32)
    tall = jax.ShapeDtypeStruct((expand // 128, count, 128), F32)
    four_tall = jax.ShapeDtypeStruct((4, expand // 128, count, 128), F32)
    four = jax.ShapeDtypeStruct((4, count, expand), F32)
    wide = jax.ShapeDtypeStruct((count, 2 * expand), F32)
    like = lambda a: jax.ShapeDtypeStruct(a.shape, a.dtype)
    pay_cols, pay_rows = (
        jax.ShapeDtypeStruct((2 * lines * expand // 128 + 8, 128), F32) for lines in (height, breadth)
    )
    order = send_order(cols, rows)
    pays = tuple(pay_cols if axis == "cols" else pay_rows for axis, _, _ in order)
    outs = vmem_call(
        functools.partial(edges_body, order),
        (*pays, like(pixels), like(cotangent), like(decay_rates), wide, full, four, four),
        scratch=[
            pltpu.VMEM(w_in.shape, BF16),
            pltpu.VMEM(w_out.shape, BF16),
            pltpu.VMEM(step_sizes.shape, F32),
            *(pltpu.VMEM(tall.shape, F32) for _ in range(4)),
            pltpu.VMEM((2, 2, *pay_cols.shape), F32),
            pltpu.SemaphoreType.DMA((6,)),
        ],
        given=pltpu.HBM,
    )(pixels, cotangent, w_in, w_out, decay_rates, step_sizes)
    sent = outs[: len(pays)]
    px, ct, rt, mixed, back, dec, wgt = outs[len(pays) :]
    turned = jax.ShapeDtypeStruct((channels, count), BF16)
    s_loc, g_loc, pre, suf, m_in, m_gate, gated, x_t, c_t = vmem_call(
        local_body,
        (tall, tall, four_tall, four_tall, full, full, full, turned, turned),
        scratch=[pltpu.VMEM(tall.shape, F32)] * 2,
    )(px, ct, mixed, back, dec, wgt)
    received = {key: transfer(payload, *key) for key, payload in zip(order, sent)}
    split = rows == 4 and cols == 4 and channels == 128 and expand == 256
    if split:
        grads = (jax.ShapeDtypeStruct((4, 4, 48, 128), F32),)
    else:
        grads = (
            jax.ShapeDtypeStruct((channels, 2 * expand), F32),
            jax.ShapeDtypeStruct((channels, expand), F32),
        )
    outs = vmem_call(
        functools.partial(join_body, (height, breadth), split, order),
        (jax.ShapeDtypeStruct((count, 2 * expand), BF16), *grads),
        scratch=[pltpu.VMEM((count, expand), BF16)],
    )(rt, *received.values(), s_loc, g_loc, pre, suf, m_in, m_gate, gated, x_t, c_t)
    mix, grads = outs[0], outs[1:]
    grad_pixels = vmem_call(pixels_body, like(pixels), kept=False)(ct, mix, w_in)
    if split:
        parts = spread(grads[0], "cols", [("shift", k) for k in (1, 2, 3)])
        value = (parts[0] + parts[1]) + (parts[2] + parts[3])
        parts = spread(value, "rows", [("shift", k) for k in (1, 2, 3)])
        grad_in, grad_out = vmem_call(
            final_body, (jax.ShapeDtypeStruct((32, 128), F32), jax.ShapeDtypeStruct((32, 64), F32)), kept=False
        )(*parts)
        return grad_pixels, grad_in, jnp.transpose(grad_out)
    full_in, full_out = grads[0], jnp.transpose(grads[1])
    full_in = lax.psum_scatter(full_in, "cols", scatter_dimension=1, tiled=True)
    full_out = lax.psum_scatter(full_out, "cols", scatter_dimension=1, tiled=True)
    return (
        grad_pixels,
        lax.psum_scatter(full_in, "rows", scatter_dimension=0, tiled=True),
        lax.psum_scatter(full_out, "rows", scatter_dimension=0, tiled=True),
    )


def solution(mesh):
    return jax.shard_map(
        per_device,
        mesh=mesh,
        in_specs=(
            P(("groups", "rows"), "cols", None),
            P(("groups", "rows"), "cols", None),
            P(),
            P(),
            P(),
            P(None, ("groups", "rows"), "cols"),
        ),
        out_specs=(
            P(("groups", "rows"), "cols", None),
            P(("groups", "rows"), "cols"),
            P(("groups", "rows"), "cols"),
        ),
        check_vma=False,
    )
```

```python
import functools

import jax
import jax.numpy as jnp
from jax import lax
from jax.experimental import pallas as pl
from jax.experimental.pallas import tpu as pltpu
from jax.sharding import PartitionSpec as P

F32 = jnp.float32
BF16 = jnp.bfloat16
contract_rows = (((0,), (0,)), ((), ()))
contract_cols = (((1,), (1,)), ((), ()))
VMEM_LIMIT = 6 * 1024 * 1024


def vmem_call(body, out_shape, scratch=(), given=pltpu.VMEM, kept=True):
    spec = pl.BlockSpec(memory_space=pltpu.VMEM)
    if kept:
        out_shape = jax.tree.map(lambda s: pltpu.VMEM(s.shape, s.dtype), out_shape)

    def call(*operands):
        operands = [pltpu.with_memory_space_constraint(a, given) for a in operands]
        return pl.pallas_call(
            body,
            out_shape=out_shape,
            in_specs=[pl.BlockSpec(memory_space=given)] * len(operands),
            out_specs=jax.tree.map(lambda _: spec, out_shape),
            scratch_shapes=scratch,
            compiler_params=pltpu.CompilerParams(vmem_limit_bytes=VMEM_LIMIT),
            cost_estimate=pl.CostEstimate(flops=0, bytes_accessed=0, transcendentals=0),
        )(*operands)

    return call


def get(ref, rows):
    return jnp.concatenate([ref[k, rows, :] for k in range(ref.shape[0])], axis=1)


def put(ref, rows, value):
    for k in range(ref.shape[0]):
        ref[k, rows, :] = value[:, 128 * k : 128 * k + 128]


def sigmoid(value):
    return 0.5 * jnp.tanh(0.5 * value) + 0.5


def decay_pair(rate, step):
    decay = jnp.exp(-(rate * step))
    rest = 1.0 - decay * decay
    return decay, rest * lax.rsqrt(rest)


def pack_column(column):
    pieces = column.shape[0] // 8
    lane = lax.broadcasted_iota(jnp.int32, (8, 128), 1)
    packed = jnp.broadcast_to(column[0:8], (8, 128))
    for k in range(1, pieces):
        packed = jnp.where(lane < k * (128 // pieces), packed, column[8 * k : 8 * k + 8])
    return packed


def pack_states(out, one, two):
    lines = one.shape[0]
    both = jnp.concatenate([one, two], axis=1)
    for k in range(both.shape[1] // 128):
        out[k * lines : (k + 1) * lines, :] = both[:, 128 * k : 128 * k + 128]


def unpack(part, lines, expand):
    tiles = 2 * expand // 128
    states = jnp.concatenate([part[k * lines : (k + 1) * lines, :] for k in range(tiles)], axis=1)
    packed = part[tiles * lines :, :]
    pieces = 2 * lines // 8
    columns = [
        jnp.broadcast_to(packed[:, k * (128 // pieces) : k * (128 // pieces) + 1], (8, expand)) for k in range(pieces)
    ]
    half = pieces // 2
    sums = [jnp.concatenate(columns[d * half : (d + 1) * half], axis=0) for d in (0, 1)]
    return states, jnp.concatenate(sums, axis=1)


def edges_body(order, px_in, ct_in, wi_in, wo_in, rt_in, ss_in, *refs):
    sent = refs[: len(order)]
    px, ct, rt, mixed, back, dec, wgt, wi, wo, ss, src, seed, src_lines, seed_lines, ways, sems = refs[len(order) :]
    pairs = ((wi_in, wi), (px_in, px), (ct_in, ct), (wo_in, wo), (ss_in, ss), (rt_in, rt))
    copies = [pltpu.make_async_copy(a, b, sems.at[k]) for k, (a, b) in enumerate(pairs)]
    for copy in copies:
        copy.start()
    height, breadth, channels = px.shape
    expand = wo.shape[0]
    count = height * breadth
    for copy in copies:
        copy.wait()
    for axis, length, lines in ((0, breadth, height), (1, height, breadth)):
        one, two = 2 * axis, 2 * axis + 1
        steps = {d: ss[d] if axis == 0 else jnp.transpose(ss[d]) for d in (one, two)}
        for i in range(length):
            rows = slice(i * lines, (i + 1) * lines)
            for d, step in steps.items():
                dec[d, rows, :], wgt[d, rows, :] = decay_pair(rt[d : d + 1, :], step[:, i : i + 1])
        sums = jnp.concatenate([jnp.sum(step, axis=1, keepdims=True) for step in steps.values()], axis=0)
        for way in (0, 1):
            ways[axis, way, 2 * lines * expand // 128 :, :] = pack_column(sums)
    both = jnp.dot(px[...].reshape(count, channels), wi[...], preferred_element_type=F32)
    mixed[...] = both
    inner, gate = both[:, :expand], both[:, expand:]
    put(src, slice(None), inner * sigmoid(inner))
    cot = ct[...].reshape(count, channels)
    bg = lax.dot_general(cot, wo[...], contract_cols, preferred_element_type=F32)
    back[...] = bg
    put(seed, slice(None), bg * (gate * sigmoid(gate)))
    for axis, name in ((0, "cols"), (1, "rows")):
        payload = ways.at[axis]
        one, two = 2 * axis, 2 * axis + 1
        length = breadth if axis == 0 else height
        lines = height if axis == 0 else breadth

        if axis == 0:
            source, grad = src_lines, seed_lines
        else:
            source, grad = src, seed

        fwd = jnp.zeros((lines, expand), F32)
        adj = jnp.zeros((lines, expand), F32)
        for i in range(length):
            rows = slice(i * lines, (i + 1) * lines)
            if axis == 0:
                for ref, line_ref in ((src, src_lines), (seed, seed_lines)):
                    put(line_ref, rows, get(ref, pl.ds(i, lines, stride=length)))
            fwd = dec[one, rows, :] * fwd + wgt[one, rows, :] * get(source, rows)
            adj = dec[two, rows, :] * (adj + get(grad, rows))
        pack_states(payload.at[0], fwd, adj)
        fwd = jnp.zeros((lines, expand), F32)
        adj = jnp.zeros((lines, expand), F32)
        for i in reversed(range(length)):
            rows = slice(i * lines, (i + 1) * lines)
            fwd = dec[two, rows, :] * fwd + wgt[two, rows, :] * get(source, rows)
            adj = dec[one, rows, :] * (adj + get(grad, rows))
        pack_states(payload.at[1], adj, fwd)
        mine, count_of = lax.axis_index(name), 1 + sum(key[0] == name for key in order)
        for (out_axis, kind, k), out in zip(order, sent):
            if out_axis == name:
                out[...] = payload[(target(mine, kind, k, count_of) < mine).astype(jnp.int32)]


def local_body(px, ct, mixed, back, dec, wgt, s_loc, g_loc, pre, suf, m_in, m_gate, gated, x_t, c_t, src, seed):
    height, breadth, channels = px.shape
    expand = src.shape[0] * 128
    count = height * breadth
    inner, gate = mixed[:, :expand], mixed[:, expand:]
    s_in, s_gate = sigmoid(inner), sigmoid(gate)
    gate_silu = gate * s_gate
    put(src, slice(None), inner * s_in)
    put(seed, slice(None), back[...] * gate_silu)
    m_in[...] = s_in * (1.0 + inner * (1.0 - s_in))
    gated[...] = gate_silu
    m_gate[...] = back[...] * (s_gate * (1.0 + gate * (1.0 - s_gate)))
    x_t[...] = jnp.transpose(px[...].reshape(count, channels).astype(F32)).astype(BF16)
    c_t[...] = jnp.transpose(ct[...].reshape(count, channels).astype(F32)).astype(BF16)
    for axis in (0, 1):
        one, two = 2 * axis, 2 * axis + 1
        length = breadth if axis == 0 else height
        lines = height if axis == 0 else breadth

        def where(i):
            if axis == 0:
                return pl.ds(i, lines, stride=length)
            return pl.ds(i * lines, lines)

        def go(order, a, b, first):
            state = jnp.zeros((lines, expand), F32)
            carried = jnp.zeros((lines, expand), F32)
            upto = jnp.ones((lines, expand), F32)
            after = jnp.ones((lines, expand), F32)
            for i in order:
                rows = slice(i * lines, (i + 1) * lines)
                da, wa, db, wb = dec[a, rows, :], wgt[a, rows, :], dec[b, rows, :], wgt[b, rows, :]
                state = da * state + wa * get(src, where(i))
                upto = upto * da
                adjoint = get(seed, where(i)) + carried
                carried = db * adjoint
                put(pre.at[a], where(i), upto)
                put(suf.at[b], where(i), wb * after)
                after = after * db
                grad = wb * adjoint
                if not first:
                    state_sum, grad = get(s_loc, where(i)) + state, get(g_loc, where(i)) + grad
                else:
                    state_sum = state
                put(s_loc, where(i), state_sum)
                put(g_loc, where(i), grad)

        go(range(length), one, two, axis == 0)
        go(reversed(range(length)), two, one, False)


def target(mine, kind, k, count):
    if kind == "xor":
        return mine ^ k
    place = mine + k
    return jnp.where(place < count, place, place - count)


def entering(axis, rates, received):
    keys = [key for key in received if key[0] == axis]
    parts = [received[key] for key in keys]
    count, mine = len(parts) + 1, lax.axis_index(axis)
    expand = rates[0].shape[1]
    lines = (parts[0].shape[0] - 8) * 128 // (2 * expand)
    parts, sums = zip(*(unpack(part, lines, expand) for part in parts))
    places = [target(mine, kind, k if kind == "xor" else count - k, count) for _, kind, k in keys]
    both = jnp.concatenate(rates, axis=1)
    below = jnp.zeros((lines, 2 * expand), F32)
    above = jnp.zeros((lines, 2 * expand), F32)
    for k, place in enumerate(places):
        between = jnp.zeros((lines, 2 * expand), F32)
        for m, middle in enumerate(places):
            if m != k:
                inside = ((middle - mine) * (middle - place) < 0).astype(F32)
                between = between + inside * sums[m]
        value = jnp.exp(-both * between) * parts[k]
        lower = (place < mine).astype(F32)
        below = below + lower * value
        above = above + (1.0 - lower) * value
    return below, above


def join_body(shape, split, order, rt, *refs):
    height, breadth = shape
    received = {key: ref[...] for key, ref in zip(order, refs)}
    s_loc, g_loc, pre, suf, m_in, m_gate, gated, x_t, c_t, mix = refs[len(order) : len(order) + 10]
    *grads, out_state = refs[len(order) + 10 :]
    expand = s_loc.shape[0] * 128
    rates = [rt[d : d + 1, :] for d in range(4)]
    below, above = entering("rows", rates[2:], received)
    f2, a3, a2, f3 = below[:, :expand], below[:, expand:], above[:, :expand], above[:, expand:]
    below, above = entering("cols", rates[:2], received)
    for h in range(height):
        rows = slice(h * breadth, (h + 1) * breadth)
        f0, a1 = below[h : h + 1, :expand], below[h : h + 1, expand:]
        a0, f1 = above[h : h + 1, :expand], above[h : h + 1, expand:]
        total, grad = get(s_loc, rows), get(g_loc, rows)
        for d, (state_in, adjoint_in) in enumerate(((f0, a0), (f1, a1), (f2, a2), (f3, a3))):
            total = total + get(pre.at[d], rows) * state_in
            grad = grad + get(suf.at[d], rows) * adjoint_in
        out_state[rows, :] = (total * gated[rows, :]).astype(BF16)
        mix[rows, :expand] = (grad * m_in[rows, :]).astype(BF16)
        mix[rows, expand:] = (total * m_gate[rows, :]).astype(BF16)
    grad_in = jnp.dot(x_t[...], mix[...], preferred_element_type=F32)
    grad_out = jnp.dot(c_t[...], out_state[...], preferred_element_type=F32)
    if not split:
        grads[0][...] = grad_in
        grads[1][...] = grad_out
        return
    packed = grads[0]
    lane = lax.broadcasted_iota(jnp.int32, (16, 128), 1)
    for c in range(4):
        for t in range(2):
            top = grad_out[32 * c : 32 * c + 16, 128 * t : 128 * t + 128]
            bottom = grad_out[32 * c + 16 : 32 * c + 32, 128 * t : 128 * t + 128]
            low = jnp.where(lane < 64, top, pltpu.roll(bottom, 64, 1))
            high = jnp.where(lane < 64, pltpu.roll(top, 64, 1), bottom)
            for k, piece in ((0, low), (1, high)):
                r = 2 * t + k
                packed[c, r, 0:32, :] = grad_in[32 * r : 32 * r + 32, 128 * c : 128 * c + 128]
                packed[c, r, 32:48, :] = piece


def pixels_body(ct, mix, wi, out):
    height, breadth, channels = ct.shape
    grad = lax.dot_general(mix[...], wi[...], contract_cols, preferred_element_type=F32)
    cot = ct[...].reshape(height * breadth, channels).astype(F32)
    out[...] = (cot + grad).astype(BF16).reshape(height, breadth, channels)


def final_body(mine, one, two, three, g_in, g_out):
    total = (mine[...] + one[...]) + (two[...] + three[...])
    g_in[...] = total[0:32, :]
    g_out[0:16, :] = total[32:48, 0:64]
    g_out[16:32, :] = total[32:48, 64:128]


def send_order(cols, rows):
    near = sorted(range(1, rows), key=lambda k: min(k, rows - k))
    return [("rows", "shift", k) for k in near] + [("cols", "xor", k) for k in reversed(range(1, cols))]


def transfer(value, axis, kind, k):
    count = lax.axis_size(axis)
    return lax.ppermute(value, axis, [(i, i ^ k if kind == "xor" else (i + k) % count) for i in range(count)])


def spread(value, axis, order):
    count, mine = lax.axis_size(axis), lax.axis_index(axis)
    pick = lambda i: lax.dynamic_index_in_dim(value, i, 0, keepdims=False)
    return [pick(mine)] + [transfer(pick(target(mine, kind, k, count)), axis, kind, k) for kind, k in order]


def per_device(pixels, cotangent, w_in, w_out, decay_rates, step_sizes):
    height, breadth, channels = pixels.shape
    expand = w_out.shape[0]
    count = height * breadth
    rows, cols = lax.axis_size("rows"), lax.axis_size("cols")
    full = jax.ShapeDtypeStruct((count, expand), F32)
    tall = jax.ShapeDtypeStruct((expand // 128, count, 128), F32)
    four_tall = jax.ShapeDtypeStruct((4, expand // 128, count, 128), F32)
    four = jax.ShapeDtypeStruct((4, count, expand), F32)
    wide = jax.ShapeDtypeStruct((count, 2 * expand), F32)
    like = lambda a: jax.ShapeDtypeStruct(a.shape, a.dtype)
    pay_cols, pay_rows = (
        jax.ShapeDtypeStruct((2 * lines * expand // 128 + 8, 128), F32) for lines in (height, breadth)
    )
    order = send_order(cols, rows)
    pays = tuple(pay_cols if axis == "cols" else pay_rows for axis, _, _ in order)
    outs = vmem_call(
        functools.partial(edges_body, order),
        (*pays, like(pixels), like(cotangent), like(decay_rates), wide, full, four, four),
        scratch=[
            pltpu.VMEM(w_in.shape, BF16),
            pltpu.VMEM(w_out.shape, BF16),
            pltpu.VMEM(step_sizes.shape, F32),
            *(pltpu.VMEM(tall.shape, F32) for _ in range(4)),
            pltpu.VMEM((2, 2, *pay_cols.shape), F32),
            pltpu.SemaphoreType.DMA((6,)),
        ],
        given=pltpu.HBM,
    )(pixels, cotangent, w_in, w_out, decay_rates, step_sizes)
    sent = outs[: len(pays)]
    px, ct, rt, mixed, back, dec, wgt = outs[len(pays) :]
    turned = jax.ShapeDtypeStruct((channels, count), BF16)
    s_loc, g_loc, pre, suf, m_in, m_gate, gated, x_t, c_t = vmem_call(
        local_body,
        (tall, tall, four_tall, four_tall, full, full, full, turned, turned),
        scratch=[pltpu.VMEM(tall.shape, F32)] * 2,
    )(px, ct, mixed, back, dec, wgt)
    received = {key: transfer(payload, *key) for key, payload in zip(order, sent)}
    split = rows == 4 and cols == 4 and channels == 128 and expand == 256
    if split:
        grads = (jax.ShapeDtypeStruct((4, 4, 48, 128), F32),)
    else:
        grads = (
            jax.ShapeDtypeStruct((channels, 2 * expand), F32),
            jax.ShapeDtypeStruct((channels, expand), F32),
        )
    outs = vmem_call(
        functools.partial(join_body, (height, breadth), split, order),
        (jax.ShapeDtypeStruct((count, 2 * expand), BF16), *grads),
        scratch=[pltpu.VMEM((count, expand), BF16)],
    )(rt, *received.values(), s_loc, g_loc, pre, suf, m_in, m_gate, gated, x_t, c_t)
    mix, grads = outs[0], outs[1:]
    grad_pixels = vmem_call(pixels_body, like(pixels), kept=False)(ct, mix, w_in)
    if split:
        parts = spread(grads[0], "cols", [("shift", k) for k in (1, 2, 3)])
        value = (parts[0] + parts[1]) + (parts[2] + parts[3])
        parts = spread(value, "rows", [("shift", k) for k in (1, 2, 3)])
        grad_in, grad_out = vmem_call(
            final_body, (jax.ShapeDtypeStruct((32, 128), F32), jax.ShapeDtypeStruct((32, 64), F32)), kept=False
        )(*parts)
        return grad_pixels, grad_in, jnp.transpose(grad_out)
    full_in, full_out = grads[0], jnp.transpose(grads[1])
    full_in = lax.psum_scatter(full_in, "cols", scatter_dimension=1, tiled=True)
    full_out = lax.psum_scatter(full_out, "cols", scatter_dimension=1, tiled=True)
    return (
        grad_pixels,
        lax.psum_scatter(full_in, "rows", scatter_dimension=0, tiled=True),
        lax.psum_scatter(full_out, "rows", scatter_dimension=0, tiled=True),
    )


def solution(mesh):
    return jax.shard_map(
        per_device,
        mesh=mesh,
        in_specs=(
            P(("groups", "rows"), "cols", None),
            P(("groups", "rows"), "cols", None),
            P(),
            P(),
            P(),
            P(None, ("groups", "rows"), "cols"),
        ),
        out_specs=(
            P(("groups", "rows"), "cols", None),
            P(("groups", "rows"), "cols"),
            P(("groups", "rows"), "cols"),
        ),
        check_vma=False,
    )
```
